128 devices in a mesh: ctx: 16 (over y, z), ch: 8 (over x, core).
Axes of the slice: x: 4, y: 4, z: 4, core: 2. Of those that a mesh axis runs over, the one named last changes fastest.
Arguments:
- streams: bfloat16 [3, 3, 8192, 4096], P(None, None, 'ctx', 'ch'), may hold values from -6 to 6
- short_filter: float32 [3, 7, 256], P(None, None, 'ch'), may hold values from -2 to 2
- medium_filter: bfloat16 [128, 256], P(None, 'ch'), may hold values from -0.5 to 0.5
- rates: float32 [16, 256], P(None, 'ch'), as said below
- residues: float32 [16, 256], P(None, 'ch'), may hold values from -1 to 1
- cotangent: bfloat16 [3, 8192, 4096], P(None, 'ctx', 'ch'), may hold values from -60 to 60
Outputs:
- filtered: bfloat16 [3, 8192, 4096], P(None, 'ctx', 'ch')
- stream_grads: bfloat16 [3, 3, 8192, 4096], P(None, None, 'ctx', 'ch')
- short_grad: float32 [3, 7, 256], P(None, None, 'ch')
- medium_grad: float32 [128, 256], P(None, 'ch')
The draws below stay inside these ranges and needn't reach their ends.
Inputs may be any that keep to these rules, and one draw needn't show every extreme that they name: `rates`: decay rate of each pole, between 0 and 1/30; the pole is exp(-rate).
All inputs are finite; a program needn't handle non-finite values.
Results may differ from the reference program's by a relative error of at most 0.0056.
Values may be sent and summed in bfloat16 or wider, within the bound.
A program may use at most 192 MiB of HBM per device.

```python
import jax
import jax.numpy as jnp
from jax import lax

D = 4096
GROUP = 16
SHORT = 7
MEDIUM = 128
POLES = 16
SEQS = 3
GROUPS = 256
L = 8192


def modal_parts(key):
    subkeys = jax.random.split(jax.random.fold_in(key, 29), 5)
    slow_share = 0.4
    middle_share = 0.35
    picker = jax.random.uniform(subkeys[0], (POLES, GROUPS))
    slow_rate = jnp.exp(jax.random.uniform(subkeys[1], (POLES, GROUPS), minval=jnp.log(0.2 / L), maxval=jnp.log(2.0 / L)))
    fast_rate = jnp.exp(jax.random.uniform(subkeys[2], (POLES, GROUPS), minval=jnp.log(1.0 / 50.0), maxval=jnp.log(1.0 / 30.0)))
    middle_rate = jnp.exp(jax.random.uniform(subkeys[4], (POLES, GROUPS), minval=jnp.log(1.0 / 2000.0), maxval=jnp.log(1.0 / 100.0)))
    rates = jnp.where(picker < slow_share, slow_rate, jnp.where(picker < slow_share + middle_share, middle_rate, fast_rate))
    residues = jnp.clip(jax.random.normal(subkeys[3], (POLES, GROUPS)), -4.0, 4.0) * jnp.sqrt(2.0 * rates) * 0.5
    return (rates, residues)


def draw_rates(key, part):
    return modal_parts(key)[0].astype(jnp.float32)


def draw_residues(key, part):
    return modal_parts(key)[1].astype(jnp.float32)


def draw_cotangent(key, part):
    subkeys = jax.random.split(jax.random.fold_in(key, 11), 3)
    row_pos = jnp.arange(L, dtype=jnp.float32) / L
    col_pos = jnp.arange(D, dtype=jnp.float32) / D
    row_scale = jnp.exp(jnp.log(4.0) * row_pos)[None, :] * jnp.exp(jax.random.uniform(subkeys[0], (SEQS, L), minval=0.0, maxval=jnp.log(3.0)))
    col_scale = jnp.exp(jnp.log(3.0) * col_pos) * jnp.exp(jax.random.uniform(subkeys[1], (D,), minval=0.0, maxval=jnp.log(3.0)))
    values = jnp.clip(jax.random.normal(subkeys[2], (SEQS, L, D)), -4.0, 4.0)
    return (values * row_scale[:, :, None] * col_scale[None, None, :] / 8.0).astype(jnp.bfloat16)


def levels(key, shape, shards, low, largest):
    def one(position, blocks):
        steps = jax.random.uniform(jax.random.fold_in(jax.random.fold_in(key, 6), position), (blocks,), jnp.float32, low / len(shards), largest / len(shards))
        return jnp.repeat(jnp.exp(steps), shape[position] // blocks).reshape((-1,) + (1,) * (len(shape) - position - 1))

    loudness = one(*shards[0])
    for cut in shards[1:]:
        loudness = loudness * one(*cut)
    return loudness


def normal_values(stream_key, shape, scale, reach, cuts=(), held_as=jnp.bfloat16):
    array = jax.random.normal(stream_key, shape, jnp.float32) * scale
    if len(cuts) > 0:
        array = levels(stream_key, shape, cuts, -0.22, 0.18) * array
    return jnp.clip(array, min=-reach, max=reach).astype(held_as)


def setup_inputs(seed: int = 0) -> dict:
    arg_keys = jax.random.split(jax.random.key(seed), 7)
    streams = normal_values(arg_keys[0], (3, SEQS, L, D), 1.0, 6.0, ((2, 16), (3, 8)))
    short_filter = normal_values(arg_keys[1], (3, SHORT, GROUPS), SHORT ** -0.5, 2.0, ((2, 8),), jnp.float32)
    medium_filter = normal_values(arg_keys[2], (MEDIUM, GROUPS), MEDIUM ** -0.5, 0.5, ((1, 8),))
    rates = draw_rates(jax.random.fold_in(arg_keys[6], 71), 0)
    residues = draw_residues(jax.random.fold_in(arg_keys[6], 71), 0)
    cotangent = draw_cotangent(jax.random.fold_in(arg_keys[6], 71), 0)
    return dict(streams=streams, short_filter=short_filter, medium_filter=medium_filter, rates=rates, residues=residues, cotangent=cotangent)


clip_norm = 100.0

def expand_groups(table):
    return jnp.repeat(table, GROUP, axis=-1)

def band_matrix(medium_filter):
    groups = medium_filter.shape[1]
    reverse = jnp.flip(medium_filter, 0).T
    line_vec = jnp.concatenate([jnp.zeros((groups, 1), reverse.dtype), reverse, jnp.zeros((groups, MEDIUM), reverse.dtype)], axis=1)
    tiled = jnp.tile(line_vec, (1, MEDIUM))[:, :2 * MEDIUM * MEDIUM]
    return tiled.reshape(groups, MEDIUM, 2 * MEDIUM)

def causal_taps(values, short_taps):
    summed = jnp.zeros(values.shape, jnp.float32)
    for offset in range(SHORT):
        moved = jnp.pad(values, ((offset, 0), (0, 0)))[:values.shape[0]]
        summed = summed + short_taps[offset][None, :] * moved.astype(jnp.float32)
    return summed

def anticausal_taps(values, short_taps):
    summed = jnp.zeros(values.shape, jnp.float32)
    for offset in range(SHORT):
        moved = jnp.pad(values, ((0, offset), (0, 0)))[offset:]
        summed = summed + short_taps[offset][None, :] * moved
    return summed

def split_blocks(values):
    return values.reshape(L // MEDIUM, MEDIUM, values.shape[1] // GROUP, GROUP).astype(jnp.float32)

def with_before(blocks):
    before = jnp.concatenate([jnp.zeros_like(blocks[:1]), blocks[:-1]], axis=0)
    return jnp.concatenate([before, blocks], axis=1)

def medium_forward(mixed_in, band_table):
    joined = with_before(split_blocks(mixed_in))
    return jnp.einsum('grs,psgc->prgc', band_table.astype(jnp.float32), joined).reshape(L, mixed_in.shape[1])

def medium_backward(grad_low, band_table):
    blocks = split_blocks(grad_low)
    after_blocks = jnp.concatenate([blocks[1:], jnp.zeros_like(blocks[:1])], axis=0)
    joined = jnp.concatenate([blocks, after_blocks], axis=1)
    flipped = jnp.concatenate([jnp.swapaxes(band_table[:, :, MEDIUM:], 1, 2), jnp.swapaxes(band_table[:, :, :MEDIUM], 1, 2)], axis=2)
    return jnp.einsum('grs,psgc->prgc', flipped.astype(jnp.float32), joined).reshape(L, grad_low.shape[1])

def medium_correlation(grad_low, mixed_in):
    grads = split_blocks(grad_low)
    joined = with_before(split_blocks(mixed_in))
    lag_table = jnp.einsum('prgc,psgc->grs', grads, joined)
    groups = lag_table.shape[0]
    row_pos = jnp.arange(MEDIUM).astype(jnp.int32)
    lag_index = (row_pos[:, None] - row_pos[None, :] + MEDIUM).astype(jnp.int32)
    chosen = jnp.take_along_axis(lag_table, jnp.broadcast_to(lag_index[None], (groups, MEDIUM, MEDIUM)), axis=2)
    return lax.optimization_barrier(jnp.sum(chosen, axis=1)).T

def modal_pass(values, decay, weights, backward):

    def advance(state, row):
        state = decay * state + row[None, :]
        return (state, lax.optimization_barrier(jnp.sum(weights * state, axis=0)))
    _, result = lax.scan(advance, jnp.zeros((POLES, values.shape[1]), jnp.float32), values, reverse=backward)
    return result

def slab_pass(stream_slab, cot_slab, short_slab, medium_slab, rate_slab, residue_slab):
    band_table = band_matrix(medium_slab)
    decay = jnp.exp(-expand_groups(rate_slab))
    weights = expand_groups(residue_slab)
    short_taps = expand_groups(short_slab)
    groups = medium_slab.shape[1]
    filtered_list = []
    grads_list = []
    short_total = jnp.zeros((3, SHORT, groups), jnp.float32)
    medium_total = jnp.zeros((MEDIUM, groups), jnp.float32)
    for sequence in range(SEQS):
        query = causal_taps(stream_slab[0, sequence], short_taps[0])
        key_rows = causal_taps(stream_slab[1, sequence], short_taps[1])
        value_rows = causal_taps(stream_slab[2, sequence], short_taps[2])
        mixed_in = (key_rows * value_rows).astype(jnp.bfloat16)
        mixed = medium_forward(mixed_in, band_table)
        long_out = modal_pass(mixed, decay, weights, False)
        filtered_list.append((query * long_out).astype(jnp.bfloat16))
        upstream = cot_slab[sequence].astype(jnp.float32)
        gated_grad = upstream * query
        query_grad = upstream * long_out
        mixed_grad = modal_pass(gated_grad, decay, weights, True)
        mixed_low = mixed_grad.astype(jnp.bfloat16)
        inner_grad = medium_backward(mixed_low, band_table)
        key_grad = inner_grad * value_rows
        value_grad = inner_grad * key_rows
        grads = (query_grad, key_grad, value_grad)
        grads_list.append(jnp.stack([anticausal_taps(grads[stream], short_taps[stream]).astype(jnp.bfloat16) for stream in range(3)]))
        short_rows = []
        for stream in range(3):
            per_offset = []
            for offset in range(SHORT):
                moved = jnp.pad(stream_slab[stream, sequence], ((offset, 0), (0, 0)))[:L].astype(jnp.float32)
                per_offset.append(lax.optimization_barrier(jnp.sum(grads[stream] * moved, axis=0)).reshape(groups, GROUP).sum(axis=1))
            short_rows.append(jnp.stack(per_offset))
        short_total = short_total + jnp.stack(short_rows)
        medium_total = medium_total + medium_correlation(mixed_low, mixed_in)
    return (jnp.stack(filtered_list, axis=0), jnp.stack(grads_list, axis=1), short_total, medium_total)

def reference(streams, short_filter, medium_filter, rates, residues, cotangent):
    slab_groups = min(16, GROUPS)
    slab_width = slab_groups * GROUP
    slab_count = GROUPS // slab_groups

    def one_slab(index, carry):
        filtered, stream_grads, short_total, medium_total = carry
        first = (index * slab_width).astype(jnp.int32)
        first_group = (index * slab_groups).astype(jnp.int32)
        stream_slab = lax.dynamic_slice_in_dim(streams, first, slab_width, axis=3)
        cot_slab = lax.dynamic_slice_in_dim(cotangent, first, slab_width, axis=2)
        short_slab = lax.dynamic_slice_in_dim(short_filter, first_group, slab_groups, axis=2)
        medium_slab = lax.dynamic_slice_in_dim(medium_filter, first_group, slab_groups, axis=1)
        rate_slab = lax.dynamic_slice_in_dim(rates, first_group, slab_groups, axis=1)
        residue_slab = lax.dynamic_slice_in_dim(residues, first_group, slab_groups, axis=1)
        part_out, part_grads, part_short, part_medium = slab_pass(stream_slab, cot_slab, short_slab, medium_slab, rate_slab, residue_slab)
        filtered = lax.dynamic_update_slice_in_dim(filtered, part_out, first, axis=2)
        stream_grads = lax.dynamic_update_slice_in_dim(stream_grads, part_grads, first, axis=3)
        short_total = lax.dynamic_update_slice_in_dim(short_total, part_short, first_group, axis=2)
        medium_total = lax.dynamic_update_slice_in_dim(medium_total, part_medium, first_group, axis=1)
        return (filtered, stream_grads, short_total, medium_total)
    start = (jnp.zeros((SEQS, L, D), jnp.bfloat16), jnp.zeros((3, SEQS, L, D), jnp.bfloat16), jnp.zeros((3, SHORT, GROUPS), jnp.float32), jnp.zeros((MEDIUM, GROUPS), jnp.float32))
    filtered, stream_grads, short_total, medium_total = lax.fori_loop(jnp.int32(0), jnp.int32(slab_count), one_slab, start)
    total_norm = jnp.sqrt(jnp.sum(short_total * short_total) + jnp.sum(medium_total * medium_total))
    factor = jnp.minimum(1.0, clip_norm / (total_norm + 1e-06))
    return (filtered, stream_grads, factor * short_total, factor * medium_total)
```

```python
import functools

import jax
import jax.numpy as jnp
from jax import lax
from jax.experimental import pallas as pl
from jax.experimental.pallas import tpu as pltpu
from jax.sharding import PartitionSpec as P

GROUP = 16
SHORT = 7
MEDIUM = 128
POLES = 16
LANES = 128
HALO = 8
MESH = pl.DeviceIdType.MESH
VMEM_LIMIT = 58 * 1024 * 1024

clip_norm = 100.0
highest = lax.Precision.HIGHEST
f32 = jnp.float32
bf16 = jnp.bfloat16
NN = (((1,), (0,)), ((), ()))
NT = (((1,), (1,)), ((), ()))


def matmul(a, b, dims=NN, precision=None):
    return lax.dot_general(a, b, dims, precision=precision, preferred_element_type=f32)


def group_mask(shape, row_unit, lane_unit):
    rows = lax.broadcasted_iota(jnp.int32, shape, 0) // row_unit
    lanes = lax.broadcasted_iota(jnp.int32, shape, 1) // lane_unit
    return rows == lanes


def fill_rows(rows_ref, stream_ref, prev_ref, index):
    rows_ref[index, :HALO] = prev_ref[index, 0].astype(f32)
    rows_ref[index, HALO:] = stream_ref[index, 0].astype(f32)


def front_kernel(stream_ref, prev_ref, tap_ref, cot_ref, rate_ref, short_ref, u_ref, e_ref, state_ref, rows_ref, weight_ref):
    seq = pl.program_id(1)
    length = stream_ref.shape[2]
    block = 64

    @pl.when(seq == 0)
    def _():
        step = lax.broadcasted_iota(jnp.int32, (LANES, length), 1).astype(f32)
        rate = rate_ref[...]
        for way in range(2):
            back = (length - 1.0) - step if way == 0 else step
            full = jnp.exp(-rate * back)
            high = full.astype(bf16)
            weight_ref[way, 0] = high
            weight_ref[way, 1] = (full - high.astype(f32)).astype(bf16)

    for stream in range(3):
        fill_rows(rows_ref, stream_ref, prev_ref, stream)
    u_parts = []
    e_parts = []
    for first in range(0, length, block):
        sums = []
        for stream in range(3):
            total = None
            for offset in range(SHORT):
                begin = first + HALO - offset
                term = tap_ref[stream, offset : offset + 1, :] * rows_ref[stream, begin : begin + block, :]
                total = term if total is None else total + term
            short_ref[stream, 0, first : first + block, :] = total
            sums.append(total)
        u_parts.append((sums[1] * sums[2]).astype(bf16))
        e_parts.append((cot_ref[0, first : first + block, :].astype(f32) * sums[0]).astype(bf16))
    u = jnp.concatenate(u_parts, axis=0)
    e = jnp.concatenate(e_parts, axis=0)
    u_ref[:, 0] = u.T.reshape(LANES // GROUP, GROUP, length)
    e_ref[:, 0] = e.T.reshape(LANES // GROUP, GROUP, length)
    mask = group_mask((LANES, LANES), POLES, GROUP)
    for way, value in ((0, u), (1, e)):
        every = matmul(weight_ref[way, 0], value) + matmul(weight_ref[way, 1], value)
        own = jnp.where(mask, every, 0.0).reshape(LANES // POLES, POLES, LANES).sum(axis=0)
        row = pl.multiple_of(way * 3 * POLES + seq * POLES, POLES)
        state_ref[0, pl.ds(row, POLES), :] = own


def exchange_kernel(count, state_ref, decay_ref, u_ref, e_ref, out_ref, u_halo_ref, e_halo_ref, got, scan, back, sems, halo_sems):
    me = lax.axis_index("ctx")
    after = lax.rem(me + 1, count)
    before = lax.rem(me + count - 1, count)
    barrier = pltpu.get_barrier_semaphore()
    for step in range(1, count):
        pl.semaphore_signal(barrier, inc=1, device_id={"ctx": lax.rem(me + step, count)}, device_id_type=MESH)
    pl.semaphore_wait(barrier, count - 1)
    length = u_ref.shape[3]

    def phase(source, target, first):
        copies = []
        for step in range(1, count):
            peer = lax.rem(me + step, count)
            copies.append(
                pltpu.make_async_remote_copy(
                    src_ref=source.at[peer],
                    dst_ref=target.at[me],
                    send_sem=sems.at[first, peer],
                    recv_sem=sems.at[first + 1, me],
                    device_id={"ctx": peer},
                    device_id_type=MESH,
                )
            )
        return copies

    def arrivals(source, target, first):
        for step in range(1, count):
            peer = lax.rem(me + step, count)
            pltpu.make_async_remote_copy(
                src_ref=source.at[peer],
                dst_ref=target.at[peer],
                send_sem=sems.at[first, peer],
                recv_sem=sems.at[first + 1, peer],
                device_id={"ctx": peer},
                device_id_type=MESH,
            ).wait_recv()

    sends = phase(state_ref, got, 0)
    for copy in sends:
        copy.start()
    halos = [
        pltpu.make_async_remote_copy(
            src_ref=u_ref.at[:, :, :, pl.ds(length - LANES, LANES)],
            dst_ref=u_halo_ref,
            send_sem=halo_sems.at[0],
            recv_sem=halo_sems.at[1],
            device_id={"ctx": after},
            device_id_type=MESH,
        ),
        pltpu.make_async_remote_copy(
            src_ref=e_ref.at[:, :, :, pl.ds(0, LANES)],
            dst_ref=e_halo_ref,
            send_sem=halo_sems.at[2],
            recv_sem=halo_sems.at[3],
            device_id={"ctx": before},
            device_id_type=MESH,
        ),
    ]
    for copy in halos:
        copy.start()
    got[pl.ds(me, 1)] = state_ref[pl.ds(me, 1)]
    decay = decay_ref[pl.ds(me, 1)][0]
    arrivals(state_ref, got, 0)
    forward = lax.rem(me, 4) < 2
    running = jnp.zeros_like(decay)
    ahead = []
    for source in range(count):
        ahead.append(running)
        running = decay * running + got[source]
    running = jnp.zeros_like(decay)
    behind = [None] * count
    for source in reversed(range(count)):
        behind[source] = running
        running = decay * running + got[source]
    for target in range(count):
        scan[target] = jnp.where(forward, ahead[target], behind[target])
    returns = phase(scan, back, 2)
    for copy in returns:
        copy.start()
    back[pl.ds(me, 1)] = scan[pl.ds(me, 1)]
    arrivals(scan, back, 2)
    out_ref[...] = back[...]
    for copy in sends + returns:
        copy.wait_send()
    for copy in halos:
        copy.wait()


def slanted(row, length):
    wide = jnp.broadcast_to(row, (LANES, length))
    return pltpu.roll(wide, 0, 1, stride=1, stride_axis=0).astype(bf16)


def long_kernel(edge_ref, u_ref, u_halo_ref, e_ref, e_halo_ref, carry_ref, rate_ref, residue_ref, tap_ref, back_tap_ref,
                s_ref, w_ref, lag_ref, turned_ref):
    length = u_ref.shape[3]
    half = length // 2
    per_step = u_ref.shape[0]
    rows = 3 * GROUP
    has_prev = edge_ref[0] > 0
    has_next = edge_ref[1] > 0
    turned_ref[...] = carry_ref[0].T
    mask = group_mask((rows, 3 * POLES), GROUP, POLES)

    def one(index):
        rate = rate_ref[index]
        residue = residue_ref[index]
        first = pl.multiple_of(index * GROUP, GROUP)
        carry = turned_ref[pl.ds(first, GROUP), :]
        ahead = jnp.concatenate([carry[:, : 3 * POLES]] * 3, axis=0)
        behind = jnp.concatenate([carry[:, 3 * POLES :]] * 3, axis=0)
        u_halo = jnp.where(has_prev, u_halo_ref[index].reshape(rows, LANES), jnp.zeros((), bf16))
        e_halo = jnp.where(has_next, e_halo_ref[index].reshape(rows, LANES), jnp.zeros((), bf16))
        u_own = u_ref[index].reshape(rows, length)
        e_own = e_ref[index].reshape(rows, length)
        u_ext = jnp.concatenate([u_halo, u_own], axis=1)

        def lanes(shape):
            return lax.broadcasted_iota(jnp.int32, shape, 1).astype(f32)

        edge = lanes((POLES, LANES))

        def local_state(value, back):
            full = jnp.exp(-rate * back)
            high = full.astype(bf16)
            low = (full - high.astype(f32)).astype(bf16)
            high = jnp.concatenate([high] * 3, axis=0)
            low = jnp.concatenate([low] * 3, axis=0)
            return matmul(value, high, NT) + matmul(value, low, NT)

        ahead_far = jnp.where(mask, ahead - local_state(u_halo, (LANES - 1.0) - edge), 0.0)
        behind_near = jnp.where(mask, behind, 0.0)
        behind_far = jnp.where(mask, behind - local_state(e_halo, edge), 0.0)

        back_lag = 512.0 + 0.0 * lanes((POLES, 6 * LANES)) - lanes((POLES, 6 * LANES))
        h_back = jnp.sum(jnp.where(back_lag >= 0, residue * jnp.exp(-rate * jnp.maximum(back_lag, 0.0)), 0.0), axis=0, keepdims=True)
        lag = lanes((POLES, 6 * LANES)) - LANES
        h_ahead = jnp.sum(jnp.where(lag >= 0, residue * jnp.exp(-rate * jnp.maximum(lag, 0.0)), 0.0), axis=0, keepdims=True)
        taps = tap_ref[index]
        q = matmul(jnp.broadcast_to(taps, (16, LANES)).astype(bf16), slanted(h_ahead, 6 * LANES))[:1]
        q = jnp.where(lax.broadcasted_iota(jnp.int32, q.shape, 1) >= LANES, q, 0.0)
        q = jnp.concatenate([q, jnp.zeros((1, LANES), f32)], axis=1)
        q_table = slanted(q, 7 * LANES)
        h_table = slanted(h_back, 6 * LANES)
        k_table = slanted(back_tap_ref[index], 4 * LANES)

        moment = jnp.sum(taps * jnp.exp(rate * edge), axis=1, keepdims=True)
        time = lanes((POLES, length))
        ahead_weight = residue * moment * jnp.exp(-rate * (time + 1.0))
        ahead_weight = jnp.concatenate([ahead_weight] * 3, axis=0)
        wide = lanes((POLES, length + LANES))
        behind_weight = residue * jnp.exp(rate * (wide - length))
        behind_weight = jnp.concatenate([behind_weight] * 3, axis=0)

        left = jnp.concatenate(
            [
                jnp.concatenate([jnp.zeros((rows, half), bf16), u_ext[:, : 3 * LANES]], axis=1),
                u_ext,
            ],
            axis=0,
        )
        right = jnp.concatenate([q_table[:, 512 - LANES * b : 768 - LANES * b] for b in range(5)], axis=0)
        s_local = matmul(left, right)
        s_far = matmul(ahead_far, ahead_weight, precision=highest)
        s_ref[index] = (jnp.concatenate([s_local[:rows], s_local[rows:]], axis=1) + s_far).reshape(3, GROUP, length)

        left = jnp.concatenate(
            [
                e_own,
                jnp.concatenate([e_own[:, half:], jnp.zeros((rows, half), bf16)], axis=1),
                jnp.concatenate([e_halo, jnp.zeros((rows, length - LANES), bf16)], axis=1),
            ],
            axis=0,
        )
        right = jnp.concatenate([h_table[:, 512 - LANES * b : 768 - LANES * b] for b in range(4)], axis=0)
        p_local = matmul(left, right)
        p_local = jnp.concatenate([p_local[:rows], p_local[rows : 2 * rows], p_local[2 * rows :, :LANES]], axis=1)
        p_near = matmul(behind_near, behind_weight[:, :length], precision=highest)
        p_far = matmul(behind_far, behind_weight[:, length:], precision=highest)
        p = (p_local + jnp.concatenate([p_near, p_far], axis=1)).astype(bf16)
        p_next = jnp.where(has_next, p[:, length:], jnp.zeros((), bf16))
        p = jnp.concatenate([p[:, :length], p_next], axis=1)

        left = jnp.concatenate([p[:, : 3 * LANES], p[:, half:]], axis=0)
        right = jnp.concatenate([k_table[:, 256 - LANES * b : 512 - LANES * b] for b in range(3)], axis=0)
        w = matmul(left, right)
        w_ref[index] = jnp.concatenate([w[:rows], w[rows:]], axis=1).reshape(3, GROUP, length)

        p_stack = jnp.concatenate([p[:, LANES * b : LANES * (b + 1)] for b in range(4)], axis=0)
        u_stack = jnp.concatenate([u_ext[:, LANES * b : LANES * (b + 2)] for b in range(4)], axis=0)
        table = matmul(p_stack.T, u_stack)
        total = table[LANES - 8 :]
        for tile in reversed(range(LANES // 8 - 1)):
            total = pltpu.roll(total, 2 * LANES - 8, 1) + table[8 * tile : 8 * tile + 8]
        sub = lax.broadcasted_iota(jnp.int32, total.shape, 0)
        for bit in (1, 2, 4):
            total = jnp.where((sub & bit) > 0, pltpu.roll(total, 2 * LANES - bit, 1), total)
        total = jnp.sum(total, axis=0, keepdims=True)
        lag_ref[index] = pltpu.roll(total, 2 * LANES - 1, 1)[:, :LANES]

    def body(step, carry):
        one(2 * step)
        one(2 * step + 1)
        return carry

    lax.fori_loop(0, per_step // 2, body, 0)


def back_kernel(short_ref, stream_ref, prev_ref, tap_ref, cot_ref, s_ref, w_ref, out_ref, grad_ref, head_ref, tail_ref, corr_ref,
                rows_ref, g_ref, s_rows, w_rows, acc_ref):
    chunk = pl.program_id(0)
    seq = pl.program_id(1)
    length = stream_ref.shape[2]
    block = 64

    @pl.when(seq == 0)
    def _():
        acc_ref[...] = jnp.zeros_like(acc_ref)

    for stream in range(3):
        fill_rows(rows_ref, stream_ref, prev_ref, stream)
        g_ref[stream, length:] = jnp.zeros((HALO, LANES), f32)
    s_rows[...] = s_ref[:, 0].reshape(LANES, length).T
    w_rows[...] = w_ref[:, 0].reshape(LANES, length).T
    for first in range(0, length, block):
        here = slice(first, first + block)
        s = s_rows[here]
        w = w_rows[here]
        cot = cot_ref[0, here].astype(f32)
        out_ref[0, here] = (short_ref[0, 0, here] * s).astype(bf16)
        g_ref[0, here] = cot * s
        g_ref[1, here] = w * short_ref[2, 0, here]
        g_ref[2, here] = w * short_ref[1, 0, here]
    for stream in range(3):
        head_ref[stream, 0] = g_ref[stream, :HALO]
        for first in range(0, length, block):
            total = None
            own = g_ref[stream, first : first + block]
            for offset in range(SHORT):
                term = tap_ref[stream, offset : offset + 1, :] * g_ref[stream, first + offset : first + offset + block]
                total = term if total is None else total + term
                begin = first + HALO - offset
                part = (own * rows_ref[stream, begin : begin + block]).reshape(block // 8, 8, LANES).sum(axis=0)
                acc_ref[stream, offset] += part
            grad_ref[stream, 0, first : first + block] = total.astype(bf16)
            if first + block == length:
                tail_ref[stream, 0] = total[block - HALO :]

    @pl.when(seq == pl.num_programs(1) - 1)
    def _():
        lane = lax.broadcasted_iota(jnp.int32, (LANES, LANES), 0) // GROUP + chunk * (LANES // GROUP)
        pick = jnp.where(lane == lax.broadcasted_iota(jnp.int32, (LANES, LANES), 1), 1.0, 0.0)
        sums = acc_ref[...].sum(axis=2).reshape(3 * 8, LANES)
        value = matmul(sums, pick, precision=highest)

        @pl.when(chunk == 0)
        def _():
            corr_ref[...] = value

        @pl.when(chunk > 0)
        def _():
            corr_ref[...] += value


def reduce_kernel(count, across, corr_ref, lag_ref, head_ref, corr_out, lag_out, head_out, mine, got, norm_mine, norm_got, sems, norm_sems, head_sems):
    me = lax.axis_index("ctx")
    col = lax.axis_index("ch")
    before = lax.rem(me + count - 1, count)
    barrier = pltpu.get_barrier_semaphore()
    for step in range(1, count):
        pl.semaphore_signal(barrier, inc=1, device_id={"ctx": lax.rem(me + step, count)}, device_id_type=MESH)
    for step in range(1, across):
        pl.semaphore_signal(barrier, inc=1, device_id={"ch": lax.rem(col + step, across)}, device_id_type=MESH)
    pl.semaphore_wait(barrier, count + across - 2)
    top = corr_ref.shape[0]
    mine[:top] = corr_ref[...]
    mine[top:] = lag_ref[...]

    def send(source, target, pair, axis, here, peer):
        return pltpu.make_async_remote_copy(
            src_ref=source,
            dst_ref=target.at[here],
            send_sem=pair.at[0, peer],
            recv_sem=pair.at[1, here],
            device_id={axis: peer},
            device_id_type=MESH,
        )

    copies = []
    for step in range(1, count):
        copies.append(send(mine, got, sems, "ctx", me, lax.rem(me + step, count)))
    for copy in copies:
        copy.start()
    head = pltpu.make_async_remote_copy(
        src_ref=head_ref,
        dst_ref=head_out,
        send_sem=head_sems.at[0],
        recv_sem=head_sems.at[1],
        device_id={"ctx": before},
        device_id_type=MESH,
    )
    head.start()
    got[pl.ds(me, 1)] = mine[...][None]
    for step in range(1, count):
        peer = lax.rem(me + step, count)
        send(mine, got, sems, "ctx", peer, peer).wait_recv()
    total = got[0]
    for source in range(1, count):
        total = total + got[source]
    rows = jnp.sum((total * total).reshape(total.shape[0] // 8, 8, LANES), axis=0)
    norm_mine[...] = rows
    norms = []
    for step in range(1, across):
        norms.append(send(norm_mine, norm_got, norm_sems, "ch", col, lax.rem(col + step, across)))
    for copy in norms:
        copy.start()
    norm_got[pl.ds(col, 1)] = rows[None]
    for step in range(1, across):
        peer = lax.rem(col + step, across)
        send(norm_mine, norm_got, norm_sems, "ch", peer, peer).wait_recv()
    squares = norm_got[0]
    for source in range(1, across):
        squares = squares + norm_got[source]
    norm = jnp.sqrt(jnp.sum(jnp.sum(squares, axis=1, keepdims=True), axis=0, keepdims=True))
    factor = jnp.minimum(1.0, clip_norm / (norm + 1e-06))
    corr_out[...] = total[:top] * factor
    lag_out[...] = total[top:] * factor
    for copy in copies + norms:
        copy.wait_send()
    head.wait()


def edge_kernel(edge_ref, grad_ref, tail_ref, head_ref, tap_ref, out_ref):
    has_next = edge_ref[1] > 0
    out_ref[...] = grad_ref[...]
    for stream in range(3):
        for seq in range(3):
            head = jnp.where(has_next, head_ref[stream, seq], 0.0)
            wide = jnp.concatenate([jnp.zeros((HALO, head.shape[1]), f32), head], axis=0)
            total = tail_ref[stream, seq]
            for offset in range(1, SHORT):
                total = total + tap_ref[stream, offset : offset + 1, :] * wide[offset : offset + HALO]
            low = jnp.concatenate([jnp.zeros_like(total), total], axis=0).astype(bf16)
            keep = lax.broadcasted_iota(jnp.int32, low.shape, 0) < HALO
            out_ref[stream, seq] = jnp.where(keep, grad_ref[stream, seq], low)


def params(**more):
    return pltpu.CompilerParams(vmem_limit_bytes=VMEM_LIMIT, **more)


def on_device(streams, short_filter, medium_filter, rates, residues, cotangent):
    count = lax.axis_size("ctx")
    across = lax.axis_size("ch")
    place = lax.axis_index("ctx")
    seqs, length, width = streams.shape[1:]
    groups = width // GROUP
    chunks = width // LANES
    per_chunk = LANES // GROUP
    shape = jax.ShapeDtypeStruct

    prev = lax.ppermute(streams[:, :, length - HALO :], "ctx", [(i - 1, i) for i in range(1, count)])
    taps = jnp.pad(jnp.repeat(short_filter, GROUP, axis=-1), ((0, 0), (0, 8 - SHORT), (0, 0)))
    rate_rows = rates.T
    rate_cols = rate_rows[:, :, None]
    residue_cols = residues.T[:, :, None]
    medium = medium_filter.astype(f32).T
    tap_rows = medium[:, None, :]
    back_taps = jnp.pad(jnp.flip(medium, 1), ((0, 0), (MEDIUM + 1, 2 * MEDIUM - 1)))[:, None, :]
    edges = jnp.stack([place, count - 1 - place]).astype(jnp.int32)
    decay = jnp.repeat(jnp.exp(-rates * length), GROUP, axis=-1)
    decay = jnp.tile(decay.reshape(POLES, chunks, LANES).transpose(1, 0, 2), (1, 2 * seqs, 1))

    chunk_block = lambda c, k: (0, k, 0, c)
    turned_block = lambda c, k: (c, k, 0, 0)
    stream_spec = pl.BlockSpec((3, 1, length, LANES), chunk_block)
    prev_spec = pl.BlockSpec((3, 1, HALO, LANES), chunk_block)
    tap_spec = pl.BlockSpec((3, 8, LANES), lambda c, k: (0, 0, c))
    cot_spec = pl.BlockSpec((1, length, LANES), lambda c, k: (k, 0, c))
    turned_spec = pl.BlockSpec((per_chunk, 1, GROUP, length), turned_block)

    short_sums, u, e, states = pl.pallas_call(
        front_kernel,
        grid=(chunks, seqs),
        in_specs=[stream_spec, prev_spec, tap_spec, cot_spec, pl.BlockSpec((LANES, 1), lambda c, k: (c, 0))],
        out_specs=[stream_spec, turned_spec, turned_spec, pl.BlockSpec((1, 6 * POLES, LANES), lambda c, k: (c, 0, 0))],
        out_shape=[
            shape(streams.shape, f32),
            shape((groups, seqs, GROUP, length), bf16),
            shape((groups, seqs, GROUP, length), bf16),
            shape((chunks, 6 * POLES, LANES), f32),
        ],
        scratch_shapes=[pltpu.VMEM((3, length + HALO, LANES), f32), pltpu.VMEM((2, 2, LANES, length), bf16)],
        compiler_params=params(),
        name="front",
    )(streams, prev, taps, cotangent, rate_rows.reshape(groups * POLES, 1))

    slice_rows = chunks * 6 * POLES // count
    slots = (count, slice_rows, LANES)
    vmem = pl.BlockSpec(memory_space=pltpu.VMEM)
    anywhere = pl.BlockSpec(memory_space=pl.ANY)
    halo_shape = shape((groups, seqs, GROUP, LANES), bf16)
    carry, u_halo, e_halo = pl.pallas_call(
        functools.partial(exchange_kernel, count),
        in_specs=[vmem, vmem, anywhere, anywhere],
        out_specs=[vmem, anywhere, anywhere],
        out_shape=[shape(slots, f32), halo_shape, halo_shape],
        scratch_shapes=[
            pltpu.VMEM(slots, f32),
            pltpu.VMEM(slots, f32),
            pltpu.VMEM(slots, f32),
            pltpu.SemaphoreType.DMA((4, count)),
            pltpu.SemaphoreType.DMA((4,)),
        ],
        compiler_params=pltpu.CompilerParams(collective_id=0, has_side_effects=True),
        name="exchange",
    )(states.reshape(slots), decay.reshape(slots), u, e)

    own_spec = pl.BlockSpec((per_chunk, seqs, GROUP, length), lambda c: (c, 0, 0, 0))
    halo_spec = pl.BlockSpec((per_chunk, seqs, GROUP, LANES), lambda c: (c, 0, 0, 0))
    table_spec = lambda *tail: pl.BlockSpec((per_chunk,) + tail, lambda c: (c, 0, 0))
    smem = pl.BlockSpec(memory_space=pltpu.SMEM)
    s, w, lags = pl.pallas_call(
        long_kernel,
        grid=(chunks,),
        in_specs=[
            smem, own_spec, halo_spec, own_spec, halo_spec,
            pl.BlockSpec((1, 6 * POLES, LANES), lambda c: (c, 0, 0)),
            table_spec(POLES, 1), table_spec(POLES, 1), table_spec(1, MEDIUM), table_spec(1, 4 * MEDIUM),
        ],
        out_specs=[own_spec, own_spec, table_spec(1, LANES)],
        out_shape=[
            shape((groups, seqs, GROUP, length), f32),
            shape((groups, seqs, GROUP, length), f32),
            shape((groups, 1, LANES), f32),
        ],
        scratch_shapes=[pltpu.VMEM((LANES, 6 * POLES), f32)],
        compiler_params=params(),
        name="long",
    )(edges, u, u_halo, e, e_halo, carry.reshape(chunks, 6 * POLES, LANES), rate_cols, residue_cols, tap_rows, back_taps)

    filtered, grads, heads, tails, corr = pl.pallas_call(
        back_kernel,
        grid=(chunks, seqs),
        in_specs=[stream_spec, stream_spec, prev_spec, tap_spec, cot_spec, turned_spec, turned_spec],
        out_specs=[cot_spec, stream_spec, prev_spec, prev_spec, pl.BlockSpec((24, LANES), lambda c, k: (0, 0))],
        out_shape=[
            shape(cotangent.shape, bf16),
            shape(streams.shape, bf16),
            shape((3, seqs, HALO, width), f32),
            shape((3, seqs, HALO, width), f32),
            shape((24, LANES), f32),
        ],
        scratch_shapes=[
            pltpu.VMEM((3, length + HALO, LANES), f32),
            pltpu.VMEM((3, length + HALO, LANES), f32),
            pltpu.VMEM((length, LANES), f32),
            pltpu.VMEM((length, LANES), f32),
            pltpu.VMEM((3, 8, 8, LANES), f32),
        ],
        compiler_params=params(),
        name="back",
    )(short_sums, streams, prev, taps, cotangent, s, w)

    rows = 24 + groups
    corr_sum, lag_sum, next_heads = pl.pallas_call(
        functools.partial(reduce_kernel, count, across),
        in_specs=[vmem, vmem, anywhere],
        out_specs=[vmem, vmem, anywhere],
        out_shape=[shape((24, LANES), f32), shape((groups, LANES), f32), shape(heads.shape, f32)],
        scratch_shapes=[
            pltpu.VMEM((rows, LANES), f32),
            pltpu.VMEM((count, rows, LANES), f32),
            pltpu.VMEM((8, LANES), f32),
            pltpu.VMEM((across, 8, LANES), f32),
            pltpu.SemaphoreType.DMA((2, count)),
            pltpu.SemaphoreType.DMA((2, across)),
            pltpu.SemaphoreType.DMA((2,)),
        ],
        compiler_params=pltpu.CompilerParams(collective_id=1, has_side_effects=True),
        name="reduce",
    )(corr, lags.reshape(groups, LANES), heads)

    last = length // (2 * HALO) - 1
    whole = lambda *dims: pl.BlockSpec(dims, lambda i: (0,) * len(dims))
    last_spec = pl.BlockSpec((3, seqs, 2 * HALO, width), lambda i: (0, 0, last, 0))
    grads = pl.pallas_call(
        edge_kernel,
        grid=(1,),
        in_specs=[smem, last_spec, whole(3, seqs, HALO, width), whole(3, seqs, HALO, width), whole(3, 8, width)],
        out_specs=last_spec,
        out_shape=shape(grads.shape, bf16),
        input_output_aliases={1: 0},
        compiler_params=params(),
        name="edge",
    )(edges, grads, tails, next_heads, taps)
    short_grad = corr_sum.reshape(3, 8, LANES)[:, :SHORT, :groups]
    medium_grad = jnp.flip(lag_sum.T, 0)
    return filtered, grads, short_grad, medium_grad


def solution(mesh):
    in_specs = (
        P(None, None, "ctx", "ch"),
        P(None, None, "ch"),
        P(None, "ch"),
        P(None, "ch"),
        P(None, "ch"),
        P(None, "ctx", "ch"),
    )
    out_specs = (
        P(None, "ctx", "ch"),
        P(None, None, "ctx", "ch"),
        P(None, None, "ch"),
        P(None, "ch"),
    )
    return jax.shard_map(on_device, mesh=mesh, in_specs=in_specs, out_specs=out_specs, check_vma=False)
```

```python
import functools

import jax
import jax.numpy as jnp
from jax import lax
from jax.experimental import pallas as pl
from jax.experimental.pallas import tpu as pltpu
from jax.sharding import PartitionSpec as P

GROUP = 16
SHORT = 7
MEDIUM = 128
POLES = 16
LANES = 128
HALO = 8
MESH = pl.DeviceIdType.MESH
VMEM_LIMIT = 58 * 1024 * 1024

clip_norm = 100.0
highest = lax.Precision.HIGHEST
f32 = jnp.float32
bf16 = jnp.bfloat16
NN = (((1,), (0,)), ((), ()))
NT = (((1,), (1,)), ((), ()))


def matmul(a, b, dims=NN, precision=None):
    return lax.dot_general(a, b, dims, precision=precision, preferred_element_type=f32)


def group_mask(shape, row_unit, lane_unit):
    rows = lax.broadcasted_iota(jnp.int32, shape, 0) // row_unit
    lanes = lax.broadcasted_iota(jnp.int32, shape, 1) // lane_unit
    return rows == lanes


def fill_rows(rows_ref, stream_ref, prev, index):
    rows_ref[index, :HALO] = prev
    rows_ref[index, HALO:] = stream_ref[index, 0].astype(f32)


def spread(table, chunk):
    rows = lax.broadcasted_iota(jnp.int32, (table.shape[1], LANES), 0)
    lanes = lax.broadcasted_iota(jnp.int32, (table.shape[1], LANES), 1) // GROUP + chunk * (LANES // GROUP)
    return matmul(table, jnp.where(rows == lanes, 1.0, 0.0), precision=highest)


def remote(source, target, send_sem, recv_sem, axis, peer):
    return pltpu.make_async_remote_copy(
        src_ref=source, dst_ref=target, send_sem=send_sem, recv_sem=recv_sem, device_id={axis: peer}, device_id_type=MESH
    )


def front_kernel(count, stream_ref, whole_ref, short_filter_ref, cot_ref, rate_ref,
                 short_ref, u_ref, e_ref, prev_ref, tap_ref, carry_ref, u_halo_ref, e_halo_ref,
                 rows_ref, weight_ref, filter_ref, prev_got, u_edge, e_edge, states, got, scan, back,
                 row_sems, halo_sems, sems):
    chunk = pl.program_id(0)
    seq = pl.program_id(1)
    chunks = pl.num_programs(0)
    seqs = pl.num_programs(1)
    length = stream_ref.shape[2]
    block = 64
    quarter = count // 4
    me = lax.axis_index("ctx")
    after = lax.rem(me + 1, count)
    before = lax.rem(me + count - 1, count)
    first_step = (chunk == 0) & (seq == 0)
    last_step = (chunk == chunks - 1) & (seq == seqs - 1)
    barrier = pltpu.get_barrier_semaphore()
    stream_copy = remote(whole_ref.at[:, :, pl.ds(length - HALO, HALO), :], prev_got, row_sems.at[0], row_sems.at[1], "ctx", after)

    @pl.when(first_step)
    def _():
        for step in range(1, count):
            pl.semaphore_signal(barrier, inc=1, device_id={"ctx": lax.rem(me + step, count)}, device_id_type=MESH)

    @pl.when(seq == 0)
    def _():
        filter_ref[...] = jnp.zeros_like(filter_ref)
        for stream in range(3):
            filter_ref[8 * stream : 8 * stream + SHORT] = short_filter_ref[stream]
        tap_ref[...] = spread(filter_ref[...], chunk).reshape(3, 8, LANES)
        tiled = jnp.concatenate([rate_ref[...]] * (LANES // POLES), axis=0)
        row = lax.broadcasted_iota(jnp.int32, tiled.shape, 0) // POLES + chunk * (LANES // POLES)
        lane = lax.broadcasted_iota(jnp.int32, tiled.shape, 1)
        rate = jnp.sum(jnp.where(row == lane, tiled, 0.0), axis=1, keepdims=True)
        step = lax.broadcasted_iota(jnp.int32, (LANES, length), 1).astype(f32)
        for way in range(2):
            ago = (length - 1.0) - step if way == 0 else step
            full = jnp.exp(-rate * ago)
            high = full.astype(bf16)
            weight_ref[way, 0] = high
            weight_ref[way, 1] = (full - high.astype(f32)).astype(bf16)

    @pl.when(first_step)
    def _():
        pl.semaphore_wait(barrier, count - 1)
        stream_copy.start()

    for stream in range(3):
        rows_ref[stream, HALO:] = stream_ref[stream, 0].astype(f32)
    u_parts = []
    e_parts = []
    for first in reversed(range(0, length, block)):
        if first == 0:
            @pl.when(first_step)
            def _():
                stream_copy.wait()
                for stream in range(3):
                    for one in range(3):
                        rows = prev_got[stream, one].astype(f32)
                        prev_ref[stream, one] = jnp.where(me > 0, rows, 0.0)

            for stream in range(3):
                rows_ref[stream, :HALO] = prev_ref[stream, seq, :, pl.ds(pl.multiple_of(chunk * LANES, LANES), LANES)]
        sums = []
        for stream in range(3):
            total = None
            for offset in range(SHORT):
                begin = first + HALO - offset
                term = tap_ref[stream, offset : offset + 1, :] * rows_ref[stream, begin : begin + block, :]
                total = term if total is None else total + term
            short_ref[stream, 0, first : first + block, :] = total
            sums.append(total)
        u_parts.insert(0, (sums[1] * sums[2]).astype(bf16))
        e_parts.insert(0, (cot_ref[0, first : first + block, :].astype(f32) * sums[0]).astype(bf16))
    u = jnp.concatenate(u_parts, axis=0)
    e = jnp.concatenate(e_parts, axis=0)
    turned = u.T.reshape(LANES // GROUP, GROUP, length)
    u_ref[:, 0] = turned
    u_edge[chunk, :, seq] = turned[:, :, length - LANES :]
    turned = e.T.reshape(LANES // GROUP, GROUP, length)
    e_ref[:, 0] = turned
    e_edge[chunk, :, seq] = turned[:, :, :LANES]
    mask = group_mask((LANES, LANES), POLES, GROUP)
    for way, value in ((0, u), (1, e)):
        every = matmul(weight_ref[way, 0], value) + matmul(weight_ref[way, 1], value)
        own = jnp.where(mask, every, 0.0).reshape(LANES // POLES, POLES, LANES).sum(axis=0)
        row = pl.multiple_of(8 * seq, 8)
        states[4 * chunk + 2 * way, pl.ds(row, 8), :] = own[:8]
        states[4 * chunk + 2 * way + 1, pl.ds(row, 8), :] = own[8:]

    def halo_copies(c):
        groups = pl.ds(pl.multiple_of(c * (LANES // GROUP), LANES // GROUP), LANES // GROUP)
        return (
            remote(u_edge.at[c], u_halo_ref.at[groups], halo_sems.at[0, c], halo_sems.at[1, c], "ctx", after),
            remote(e_edge.at[c], e_halo_ref.at[groups], halo_sems.at[2, c], halo_sems.at[3, c], "ctx", before),
        )

    @pl.when(seq == seqs - 1)
    def _():
        for part in range(4):
            peer = quarter * chunk + part

            @pl.when(peer != me)
            def _():
                remote(states.at[peer], got.at[me], sems.at[0, peer], sems.at[1, me], "ctx", peer).start()

        for copy in halo_copies(chunk):
            copy.start()

    @pl.when(last_step)
    def _():
        got[pl.ds(me, 1)] = states[pl.ds(me, 1)]
        decay = jnp.exp(-float(length) * spread(rate_ref[...], me // quarter))
        decay = jnp.where(lax.rem(me, 2) == 0, decay[:8], decay[8:])
        decay = jnp.concatenate([decay] * 3, axis=0)
        forward = lax.rem(me, 4) < 2
        for step in range(1, count):
            peer = lax.rem(me + step, count)
            remote(states.at[peer], got.at[peer], sems.at[0, peer], sems.at[1, peer], "ctx", peer).wait_recv()
        running = jnp.zeros_like(decay)
        ahead = []
        for source in range(count):
            ahead.append(running)
            running = decay * running + got[source]
        running = jnp.zeros_like(decay)
        behind = [None] * count
        for source in reversed(range(count)):
            behind[source] = running
            running = decay * running + got[source]
        for target in range(count):
            scan[target] = jnp.where(forward, ahead[target], behind[target])
        for step in range(1, count):
            peer = lax.rem(me + step, count)
            remote(scan.at[peer], back.at[me], sems.at[2, peer], sems.at[3, me], "ctx", peer).start()
        back[pl.ds(me, 1)] = scan[pl.ds(me, 1)]
        for step in range(1, count):
            peer = lax.rem(me + step, count)
            remote(scan.at[peer], back.at[peer], sems.at[2, peer], sems.at[3, peer], "ctx", peer).wait_recv()
        carry_ref[...] = back[...]
        for step in range(1, count):
            peer = lax.rem(me + step, count)
            remote(states.at[peer], got.at[me], sems.at[0, peer], sems.at[1, me], "ctx", peer).wait_send()
            remote(scan.at[peer], back.at[me], sems.at[2, peer], sems.at[3, me], "ctx", peer).wait_send()
        for c in range(4):
            for copy in halo_copies(c):
                copy.wait()


def slanted(row, first_zero=False):
    lane = lax.broadcasted_iota(jnp.int32, (LANES, LANES), 1)
    here = lane >= lax.broadcasted_iota(jnp.int32, (LANES, LANES), 0)
    tiles = []
    earlier = jnp.zeros((LANES, LANES), f32)
    for j in range(row.shape[1] // LANES):
        part = jnp.broadcast_to(row[:, LANES * j : LANES * (j + 1)], (LANES, LANES))
        moved = pltpu.roll(part, 0, 1, stride=1, stride_axis=0)
        tiles.append(jnp.where(here, moved, earlier).astype(bf16))
        earlier = moved
    return tiles, jnp.where(here, 0.0, earlier).astype(bf16)


def split(value):
    high = value.astype(bf16)
    return high, (value - high.astype(f32)).astype(bf16)


def long_kernel(u_ref, u_halo_ref, e_ref, e_halo_ref, carry_ref, rate_ref, residue_ref, tap_ref, s_ref, w_ref, lag_ref, turned_ref):
    chunk = pl.program_id(0)
    place = lax.axis_index("ctx")
    count = lax.axis_size("ctx")
    length = u_ref.shape[3]
    half = length // 2
    per_step = u_ref.shape[0]
    rows = 3 * GROUP
    has_prev = place > 0
    has_next = place < count - 1
    parts = []
    for way in range(2):
        for seq in range(3):
            parts += [carry_ref[2 * way, 8 * seq : 8 * seq + 8], carry_ref[2 * way + 1, 8 * seq : 8 * seq + 8]]
    turned_ref[...] = jnp.concatenate(parts, axis=0).T
    zero = jnp.zeros((LANES, LANES), bf16)
    eye = group_mask((POLES, POLES), 1, 1)

    def lanes(shape):
        return lax.broadcasted_iota(jnp.int32, shape, 1).astype(f32)

    def one(index):
        group = chunk * per_step + index
        pick = lax.broadcasted_iota(jnp.int32, rate_ref.shape, 1) == group
        rate = jnp.sum(jnp.where(pick, rate_ref[...], 0.0), axis=1, keepdims=True)
        residue = jnp.sum(jnp.where(pick, residue_ref[...], 0.0), axis=1, keepdims=True)
        rate_row = jnp.sum(jnp.where(eye, rate, 0.0), axis=0, keepdims=True)
        carry = turned_ref[pl.ds(pl.multiple_of(index * GROUP, GROUP), GROUP), :]
        ahead = jnp.concatenate([carry[:, POLES * j : POLES * (j + 1)] for j in range(3)], axis=0)
        behind = jnp.concatenate([carry[:, POLES * j : POLES * (j + 1)] for j in range(3, 6)], axis=0)
        u_halo = jnp.where(has_prev, u_halo_ref[index].reshape(rows, LANES), jnp.zeros((), bf16))
        e_halo = jnp.where(has_next, e_halo_ref[index].reshape(rows, LANES), jnp.zeros((), bf16))
        u_own = u_ref[index].reshape(rows, length)
        e_own = e_ref[index].reshape(rows, length)
        u_ext = jnp.concatenate([u_halo, u_own], axis=1)
        edge = lanes((POLES, LANES))

        def local_state(value, ago):
            high, low = split(jnp.exp(-rate * ago))
            return matmul(jnp.concatenate([value, value], axis=1), jnp.concatenate([high, low], axis=1), NT)

        def columns(parts):
            values = [split(part) for part in parts]
            high = jnp.concatenate([value[0] for value in values], axis=0)
            low = jnp.concatenate([value[1] for value in values], axis=0)
            return jnp.concatenate([high, low, high], axis=1)

        def weights(value):
            high, low = split(value)
            return jnp.concatenate([high, high, low], axis=0)

        near = jnp.exp(-float(half) * rate_row)
        ahead = ahead - local_state(u_halo, (LANES - 1.0) - edge)
        ahead_columns = columns([ahead, ahead * near])
        far = (behind - local_state(e_halo, edge)) * jnp.exp(float(half) * rate_row)
        behind_columns = columns([behind * near, behind, far])

        lag = lanes((POLES, 5 * LANES))
        h_row = jnp.sum(residue * jnp.exp(-rate * lag), axis=0, keepdims=True)
        h_tiles, _ = slanted(h_row)
        taps = tap_ref[pl.ds(group, 1), :].astype(f32)
        q = matmul(jnp.broadcast_to(taps, (16, LANES)).astype(bf16), jnp.concatenate(h_tiles, axis=1))[:1]
        q_tiles, _ = slanted(q)
        k_tiles, k_last = slanted(taps)
        k_tile = k_tiles[0]

        moment = jnp.sum(taps * jnp.exp(rate * edge), axis=1, keepdims=True)
        time = lanes((POLES, half))
        ahead_weights = weights(residue * moment * jnp.exp(-rate * (time + 1.0)))
        behind_weights = weights(residue * jnp.exp(-rate * (half - time)))

        left = jnp.concatenate([jnp.concatenate([jnp.zeros((rows, half), bf16), u_ext[:, : 3 * LANES]], axis=1), u_ext], axis=0)
        left_tiles = [zero] + q_tiles
        right = jnp.concatenate(
            [jnp.concatenate([left_tiles[4 - b], left_tiles[5 - b]], axis=1) for b in range(5)], axis=0
        )
        s = matmul(left, right) + matmul(ahead_columns, ahead_weights)
        s_ref[index] = jnp.concatenate([s[:rows], s[rows:]], axis=1).reshape(3, GROUP, length)

        left = jnp.concatenate(
            [
                e_own,
                jnp.concatenate([e_own[:, half:], jnp.zeros((rows, half), bf16)], axis=1),
                jnp.concatenate([e_halo, jnp.zeros((rows, length - LANES), bf16)], axis=1),
            ],
            axis=0,
        )
        right = jnp.concatenate(
            [jnp.concatenate(h_tiles[:4], axis=1), jnp.concatenate([zero] + h_tiles[:3], axis=1)], axis=0
        )
        p = matmul(left, right, NT) + matmul(behind_columns, behind_weights)
        tail = jnp.where(has_next, p[2 * rows :, :LANES], 0.0)
        p = jnp.concatenate([p[:rows], p[rows : 2 * rows], tail], axis=1).astype(bf16)

        left = jnp.concatenate([p[:, : 3 * LANES], p[:, half:]], axis=0)
        right = jnp.concatenate(
            [jnp.concatenate([k_tile, k_last, zero], axis=1), jnp.concatenate([zero, k_tile, k_last], axis=1)], axis=0
        )
        w = matmul(left, right, NT)
        w_ref[index] = jnp.concatenate([w[:rows], w[rows:]], axis=1).reshape(3, GROUP, length)

        p_stack = jnp.concatenate([p[:, LANES * b : LANES * (b + 1)] for b in range(4)], axis=0)
        u_stack = jnp.concatenate([u_ext[:, LANES * b : LANES * (b + 2)] for b in range(4)], axis=0)
        table = matmul(p_stack.T, u_stack)
        total = table[LANES - 8 :]
        for tile in reversed(range(LANES // 8 - 1)):
            total = pltpu.roll(total, 2 * LANES - 8, 1) + table[8 * tile : 8 * tile + 8]
        sub = lax.broadcasted_iota(jnp.int32, total.shape, 0)
        for bit in (1, 2, 4):
            total = jnp.where((sub & bit) > 0, pltpu.roll(total, 2 * LANES - bit, 1), total)
        total = jnp.sum(total, axis=0, keepdims=True)
        lag_ref[index] = pltpu.roll(total, 2 * LANES - 1, 1)[:, :LANES]

    def body(step, carry):
        one(2 * step)
        one(2 * step + 1)
        return carry

    lax.fori_loop(0, per_step // 2, body, 0)


def back_kernel(short_ref, stream_ref, prev_ref, tap_ref, cot_ref, s_ref, w_ref, out_ref, grad_ref, head_ref, tail_ref, corr_ref,
                rows_ref, g_ref, s_rows, w_rows, acc_ref):
    chunk = pl.program_id(0)
    seq = pl.program_id(1)
    length = stream_ref.shape[2]
    block = 64

    @pl.when(seq == 0)
    def _():
        acc_ref[...] = jnp.zeros_like(acc_ref)

    for stream in range(3):
        fill_rows(rows_ref, stream_ref, prev_ref[stream, 0], stream)
        g_ref[stream, length:] = jnp.zeros((HALO, LANES), f32)
    s_rows[...] = s_ref[:, 0].reshape(LANES, length).T
    w_rows[...] = w_ref[:, 0].reshape(LANES, length).T
    for first in range(0, length, block):
        here = slice(first, first + block)
        s = s_rows[here]
        w = w_rows[here]
        cot = cot_ref[0, here].astype(f32)
        out_ref[0, here] = (short_ref[0, 0, here] * s).astype(bf16)
        g_ref[0, here] = cot * s
        g_ref[1, here] = w * short_ref[2, 0, here]
        g_ref[2, here] = w * short_ref[1, 0, here]
    for stream in range(3):
        head_ref[stream, 0] = g_ref[stream, :HALO].astype(bf16)
        for first in range(0, length, block):
            total = None
            own = g_ref[stream, first : first + block]
            for offset in range(SHORT):
                term = tap_ref[stream, offset : offset + 1, :] * g_ref[stream, first + offset : first + offset + block]
                total = term if total is None else total + term
                begin = first + HALO - offset
                part = (own * rows_ref[stream, begin : begin + block]).reshape(block // 8, 8, LANES).sum(axis=0)
                acc_ref[stream, offset] += part
            grad_ref[stream, 0, first : first + block] = total.astype(bf16)
            if first + block == length:
                tail_ref[stream, 0] = total[block - HALO :]

    @pl.when(seq == pl.num_programs(1) - 1)
    def _():
        lane = lax.broadcasted_iota(jnp.int32, (LANES, LANES), 0) // GROUP + chunk * (LANES // GROUP)
        pick = jnp.where(lane == lax.broadcasted_iota(jnp.int32, (LANES, LANES), 1), 1.0, 0.0)
        sums = acc_ref[...].sum(axis=2).reshape(3 * 8, LANES)
        value = matmul(sums, pick, precision=highest)

        @pl.when(chunk == 0)
        def _():
            corr_ref[...] = value

        @pl.when(chunk > 0)
        def _():
            corr_ref[...] += value


def reduce_kernel(count, across, corr_ref, lag_ref, head_ref, corr_out, lag_out, head_out, mine, row_got, row_sum, col_got, norm_mine, norm_got,
                  row_sems, col_sems, norm_sems, head_sems):
    inner = 4
    me = lax.axis_index("ctx")
    ch = lax.axis_index("ch")
    col = lax.rem(me, inner)
    row = me // inner
    before = lax.rem(me + count - 1, count)
    after = lax.rem(me + 1, count)
    outer = count // inner

    def in_row(step):
        place = lax.rem(col + step, inner)
        return place, row * inner + place

    def in_col(step):
        place = lax.rem(row + step, outer)
        return place, place * inner + col

    def in_ch(step):
        place = lax.rem(ch + step, across)
        return place, place

    barrier = pltpu.get_barrier_semaphore()
    peers = [in_row(step)[1] for step in range(1, inner)] + [in_col(step)[1] for step in range(1, outer)] + [before, after]
    for peer in peers:
        pl.semaphore_signal(barrier, inc=1, device_id={"ctx": peer}, device_id_type=MESH)
    for step in range(1, across):
        pl.semaphore_signal(barrier, inc=1, device_id={"ch": in_ch(step)[1]}, device_id_type=MESH)
    pl.semaphore_wait(barrier, len(peers) + across - 1)
    top = corr_ref.shape[0]
    mine[:top] = corr_ref[...]
    mine[top:] = lag_ref[...]

    def gather(source, target, sems, axis, size, here, peer_of, between=None):
        copies = []
        for step in range(1, size):
            place, peer = peer_of(step)
            copies.append(remote(source, target.at[here], sems.at[0, place], sems.at[1, here], axis, peer))
        for copy in copies:
            copy.start()
        if between is not None:
            between()
        target[pl.ds(here, 1)] = source[...][None]
        for step in range(1, size):
            place, peer = peer_of(step)
            remote(source, target.at[place], sems.at[0, place], sems.at[1, place], axis, peer).wait_recv()
        total = target[0]
        for place in range(1, size):
            total = total + target[place]
        return total, copies

    head = remote(head_ref, head_out, head_sems.at[0], head_sems.at[1], "ctx", before)
    total, sent = gather(mine, row_got, row_sems, "ctx", inner, col, in_row, head.start)
    row_sum[...] = total
    total, more = gather(row_sum, col_got, col_sems, "ctx", outer, row, in_col)
    sent = sent + more
    norm_mine[...] = jnp.sum((total * total).reshape(total.shape[0] // 8, 8, LANES), axis=0)
    squares, more = gather(norm_mine, norm_got, norm_sems, "ch", across, ch, in_ch)
    sent = sent + more
    norm = jnp.sqrt(jnp.sum(jnp.sum(squares, axis=1, keepdims=True), axis=0, keepdims=True))
    factor = jnp.minimum(1.0, clip_norm / (norm + 1e-06))
    corr_out[...] = (total[:top] * factor).reshape(3, 8, LANES)[:, :SHORT, : corr_out.shape[2]]
    turn = lax.broadcasted_iota(jnp.int32, (LANES, LANES), 0) + lax.broadcasted_iota(jnp.int32, (LANES, LANES), 1) == LANES - 1
    lag_out[...] = matmul(total[top:] * factor, jnp.where(turn, 1.0, 0.0), precision=highest)
    for copy in sent:
        copy.wait_send()
    head.wait()


def edge_kernel(grad_ref, tail_ref, head_ref, tap_ref, out_ref):
    has_next = lax.axis_index("ctx") < lax.axis_size("ctx") - 1
    for stream in range(3):
        for seq in range(3):
            head = jnp.where(has_next, head_ref[stream, seq].astype(f32), 0.0)
            wide = jnp.concatenate([jnp.zeros((HALO, head.shape[1]), f32), head], axis=0)
            total = tail_ref[stream, seq]
            for offset in range(1, SHORT):
                total = total + tap_ref[stream, offset : offset + 1, :] * wide[offset : offset + HALO]
            low = jnp.concatenate([jnp.zeros_like(total), total], axis=0).astype(bf16)
            keep = lax.broadcasted_iota(jnp.int32, low.shape, 0) < HALO
            out_ref[stream, seq] = jnp.where(keep, grad_ref[stream, seq], low)


def params(**more):
    return pltpu.CompilerParams(vmem_limit_bytes=VMEM_LIMIT, **more)


def on_device(streams, short_filter, medium_filter, rates, residues, cotangent):
    count = lax.axis_size("ctx")
    across = lax.axis_size("ch")
    seqs, length, width = streams.shape[1:]
    groups = width // GROUP
    chunks = width // LANES
    per_chunk = LANES // GROUP
    shape = jax.ShapeDtypeStruct
    vmem = pl.BlockSpec(memory_space=pltpu.VMEM)
    anywhere = pl.BlockSpec(memory_space=pl.ANY)
    whole = lambda *dims: pl.BlockSpec(dims, lambda *steps: (0,) * len(dims))

    chunk_block = lambda c, k: (0, k, 0, c)
    turned_block = lambda c, k: (c, k, 0, 0)
    stream_spec = pl.BlockSpec((3, 1, length, LANES), chunk_block)
    prev_spec = pl.BlockSpec((3, 1, HALO, LANES), chunk_block)
    tap_spec = pl.BlockSpec((3, 8, LANES), lambda c, k: (0, 0, c))
    cot_spec = pl.BlockSpec((1, length, LANES), lambda c, k: (k, 0, c))
    turned_spec = pl.BlockSpec((per_chunk, 1, GROUP, length), turned_block)
    edge_shape = (3, seqs, HALO, width)
    slots = (count, 3 * 8, LANES)
    halo_shape = shape((groups, seqs, GROUP, LANES), bf16)

    short_sums, u, e, prev, taps, carry, u_halo, e_halo = pl.pallas_call(
        functools.partial(front_kernel, count),
        grid=(chunks, seqs),
        in_specs=[stream_spec, anywhere, whole(*short_filter.shape), cot_spec, whole(*rates.shape)],
        out_specs=[
            stream_spec, turned_spec, turned_spec, whole(*edge_shape), tap_spec, whole(*slots), anywhere, anywhere,
        ],
        out_shape=[
            shape(streams.shape, f32),
            shape((groups, seqs, GROUP, length), bf16),
            shape((groups, seqs, GROUP, length), bf16),
            shape(edge_shape, f32),
            shape((3, 8, width), f32),
            shape(slots, f32),
            halo_shape,
            halo_shape,
        ],
        scratch_shapes=[
            pltpu.VMEM((3, length + HALO, LANES), f32),
            pltpu.VMEM((2, 2, LANES, length), bf16),
            pltpu.VMEM((24, groups), f32),
            pltpu.VMEM(edge_shape, bf16),
            pltpu.VMEM((chunks, per_chunk, seqs, GROUP, LANES), bf16),
            pltpu.VMEM((chunks, per_chunk, seqs, GROUP, LANES), bf16),
            pltpu.VMEM(slots, f32),
            pltpu.VMEM(slots, f32),
            pltpu.VMEM(slots, f32),
            pltpu.VMEM(slots, f32),
            pltpu.SemaphoreType.DMA((2,)),
            pltpu.SemaphoreType.DMA((4, chunks)),
            pltpu.SemaphoreType.DMA((4, count)),
        ],
        compiler_params=params(collective_id=0, has_side_effects=True),
        name="front",
    )(streams, streams, short_filter, cotangent, rates)

    own_spec = pl.BlockSpec((per_chunk, seqs, GROUP, length), lambda c: (c, 0, 0, 0))
    halo_spec = pl.BlockSpec((per_chunk, seqs, GROUP, LANES), lambda c: (c, 0, 0, 0))
    s, w, lags = pl.pallas_call(
        long_kernel,
        grid=(chunks,),
        in_specs=[
            own_spec, halo_spec, own_spec, halo_spec, pl.BlockSpec((4, 24, LANES), lambda c: (c, 0, 0)),
            whole(*rates.shape), whole(*rates.shape), whole(groups, MEDIUM),
        ],
        out_specs=[own_spec, own_spec, pl.BlockSpec((per_chunk, 1, LANES), lambda c: (c, 0, 0))],
        out_shape=[
            shape((groups, seqs, GROUP, length), f32),
            shape((groups, seqs, GROUP, length), f32),
            shape((groups, 1, LANES), f32),
        ],
        scratch_shapes=[pltpu.VMEM((LANES, 6 * POLES), f32)],
        compiler_params=params(),
        name="long",
    )(u, u_halo, e, e_halo, carry, rates, residues, medium_filter.astype(f32).T)

    filtered, grads, heads, tails, corr = pl.pallas_call(
        back_kernel,
        grid=(chunks, seqs),
        in_specs=[stream_spec, stream_spec, prev_spec, tap_spec, cot_spec, turned_spec, turned_spec],
        out_specs=[cot_spec, stream_spec, prev_spec, prev_spec, whole(24, LANES)],
        out_shape=[
            shape(cotangent.shape, bf16),
            shape(streams.shape, bf16),
            shape(edge_shape, bf16),
            shape(edge_shape, f32),
            shape((24, LANES), f32),
        ],
        scratch_shapes=[
            pltpu.VMEM((3, length + HALO, LANES), f32),
            pltpu.VMEM((3, length + HALO, LANES), f32),
            pltpu.VMEM((length, LANES), f32),
            pltpu.VMEM((length, LANES), f32),
            pltpu.VMEM((3, 8, 8, LANES), f32),
        ],
        compiler_params=params(),
        name="back",
    )(short_sums, streams, prev, taps, cotangent, s, w)

    sums = (24 + groups, LANES)
    short_grad, medium_grad, next_heads = pl.pallas_call(
        functools.partial(reduce_kernel, count, across),
        in_specs=[vmem, vmem, anywhere],
        out_specs=[vmem, vmem, anywhere],
        out_shape=[shape(short_filter.shape, f32), shape((groups, LANES), f32), shape(edge_shape, bf16)],
        scratch_shapes=[
            pltpu.VMEM(sums, f32),
            pltpu.VMEM((4,) + sums, f32),
            pltpu.VMEM(sums, f32),
            pltpu.VMEM((count // 4,) + sums, f32),
            pltpu.VMEM((8, LANES), f32),
            pltpu.VMEM((across, 8, LANES), f32),
            pltpu.SemaphoreType.DMA((2, 4)),
            pltpu.SemaphoreType.DMA((2, count // 4)),
            pltpu.SemaphoreType.DMA((2, across)),
            pltpu.SemaphoreType.DMA((2,)),
        ],
        compiler_params=pltpu.CompilerParams(collective_id=1, has_side_effects=True),
        name="reduce",
    )(corr, lags.reshape(groups, LANES), heads)

    last = length // (2 * HALO) - 1
    last_spec = pl.BlockSpec((3, seqs, 2 * HALO, width), lambda i: (0, 0, last, 0))
    grads = pl.pallas_call(
        edge_kernel,
        grid=(1,),
        in_specs=[last_spec, whole(*edge_shape), whole(*edge_shape), whole(3, 8, width)],
        out_specs=last_spec,
        out_shape=shape(grads.shape, bf16),
        input_output_aliases={0: 0},
        compiler_params=params(),
        name="edge",
    )(grads, tails, next_heads, taps)
    return filtered, grads, short_grad, medium_grad.T


def solution(mesh):
    in_specs = (
        P(None, None, "ctx", "ch"),
        P(None, None, "ch"),
        P(None, "ch"),
        P(None, "ch"),
        P(None, "ch"),
        P(None, "ctx", "ch"),
    )
    out_specs = (
        P(None, "ctx", "ch"),
        P(None, None, "ctx", "ch"),
        P(None, None, "ch"),
        P(None, "ch"),
    )
    return jax.shard_map(on_device, mesh=mesh, in_specs=in_specs, out_specs=out_specs, check_vma=False)
```

```python
import functools
from itertools import zip_longest

import jax
import jax.numpy as jnp
from jax import lax
from jax.experimental import pallas as pl
from jax.experimental.pallas import tpu as pltpu
from jax.sharding import PartitionSpec as P

GROUP = 16
SHORT = 7
MEDIUM = 128
POLES = 16
LANES = 128
HALO = 8
MESH = pl.DeviceIdType.MESH
VMEM_LIMIT = 58 * 1024 * 1024

clip_norm = 100.0
highest = lax.Precision.HIGHEST
f32 = jnp.float32
bf16 = jnp.bfloat16
NN = (((1,), (0,)), ((), ()))
NT = (((1,), (1,)), ((), ()))


def matmul(a, b, dims=NN, precision=None):
    return lax.dot_general(a, b, dims, precision=precision, preferred_element_type=f32)


def group_mask(shape, row_unit, lane_unit):
    rows = lax.broadcasted_iota(jnp.int32, shape, 0) // row_unit
    lanes = lax.broadcasted_iota(jnp.int32, shape, 1) // lane_unit
    return rows == lanes


def fill_rows(rows_ref, stream_ref, prev, index):
    rows_ref[index, :HALO] = prev
    rows_ref[index, HALO:] = stream_ref[index, 0].astype(f32)


def spread(table, chunk):
    rows = lax.broadcasted_iota(jnp.int32, (table.shape[1], LANES), 0)
    lanes = lax.broadcasted_iota(jnp.int32, (table.shape[1], LANES), 1) // GROUP + chunk * (LANES // GROUP)
    return matmul(table, jnp.where(rows == lanes, 1.0, 0.0), precision=highest)


def remote(source, target, send_sem, recv_sem, axis, peer):
    return pltpu.make_async_remote_copy(
        src_ref=source, dst_ref=target, send_sem=send_sem, recv_sem=recv_sem, device_id={axis: peer}, device_id_type=MESH
    )


def front_kernel(count, stream_ref, whole_ref, short_filter_ref, cot_ref, rate_ref,
                 short_ref, u_ref, e_ref, prev_ref, tap_ref, carry_ref, u_halo_ref, e_halo_ref,
                 rows_ref, weight_ref, filter_ref, prev_got, u_edge, e_edge, states, got, scan, back,
                 row_sems, halo_sems, sems):
    chunk = pl.program_id(0)
    seq = pl.program_id(1)
    chunks = pl.num_programs(0)
    seqs = pl.num_programs(1)
    length = stream_ref.shape[2]
    block = 64
    quarter = count // 4
    me = lax.axis_index("ctx")
    after = lax.rem(me + 1, count)
    before = lax.rem(me + count - 1, count)
    first_step = (chunk == 0) & (seq == 0)
    last_step = (chunk == chunks - 1) & (seq == seqs - 1)
    barrier = pltpu.get_barrier_semaphore()
    stream_copy = remote(whole_ref.at[:, :, pl.ds(length - HALO, HALO), :], prev_got, row_sems.at[0], row_sems.at[1], "ctx", after)

    @pl.when(first_step)
    def _():
        for step in range(1, count):
            pl.semaphore_signal(barrier, inc=1, device_id={"ctx": lax.rem(me + step, count)}, device_id_type=MESH)

    @pl.when(seq == 0)
    def _():
        filter_ref[...] = jnp.zeros_like(filter_ref)
        for stream in range(3):
            filter_ref[8 * stream : 8 * stream + SHORT] = short_filter_ref[stream]
        tap_ref[...] = spread(filter_ref[...], chunk).reshape(3, 8, LANES)
        tiled = jnp.concatenate([rate_ref[...]] * (LANES // POLES), axis=0)
        row = lax.broadcasted_iota(jnp.int32, tiled.shape, 0) // POLES + chunk * (LANES // POLES)
        lane = lax.broadcasted_iota(jnp.int32, tiled.shape, 1)
        rate = jnp.sum(jnp.where(row == lane, tiled, 0.0), axis=1, keepdims=True)
        step = lax.broadcasted_iota(jnp.int32, (LANES, length), 1).astype(f32)
        for way in range(2):
            ago = (length - 1.0) - step if way == 0 else step
            full = jnp.exp(-rate * ago)
            high = full.astype(bf16)
            weight_ref[way, 0] = high
            weight_ref[way, 1] = (full - high.astype(f32)).astype(bf16)

    @pl.when(first_step)
    def _():
        pl.semaphore_wait(barrier, count - 1)
        stream_copy.start()

    for stream in range(3):
        rows_ref[stream, HALO:] = stream_ref[stream, 0].astype(f32)
    u_parts = []
    e_parts = []
    for first in reversed(range(0, length, block)):
        if first == 0:
            @pl.when(first_step)
            def _():
                stream_copy.wait()
                for stream in range(3):
                    for one in range(3):
                        rows = prev_got[stream, one].astype(f32)
                        prev_ref[stream, one] = jnp.where(me > 0, rows, 0.0)

            for stream in range(3):
                rows_ref[stream, :HALO] = prev_ref[stream, seq, :, pl.ds(pl.multiple_of(chunk * LANES, LANES), LANES)]
        sums = []
        for stream in range(3):
            total = None
            for offset in range(SHORT):
                begin = first + HALO - offset
                term = tap_ref[stream, offset : offset + 1, :] * rows_ref[stream, begin : begin + block, :]
                total = term if total is None else total + term
            short_ref[stream, 0, first : first + block, :] = total
            sums.append(total)
        u_parts.insert(0, (sums[1] * sums[2]).astype(bf16))
        e_parts.insert(0, (cot_ref[0, first : first + block, :].astype(f32) * sums[0]).astype(bf16))
    u = jnp.concatenate(u_parts, axis=0)
    e = jnp.concatenate(e_parts, axis=0)
    turned = u.T.reshape(LANES // GROUP, GROUP, length)
    u_ref[:, 0] = turned
    u_edge[chunk, :, seq] = turned[:, :, length - LANES :]
    turned = e.T.reshape(LANES // GROUP, GROUP, length)
    e_ref[:, 0] = turned
    e_edge[chunk, :, seq] = turned[:, :, :LANES]
    mask = group_mask((LANES, LANES), POLES, GROUP)
    for way, value in ((0, u), (1, e)):
        every = matmul(weight_ref[way, 0], value) + matmul(weight_ref[way, 1], value)
        own = jnp.where(mask, every, 0.0).reshape(LANES // POLES, POLES, LANES).sum(axis=0)
        row = pl.multiple_of(8 * seq, 8)
        states[4 * chunk + 2 * way, pl.ds(row, 8), :] = own[:8]
        states[4 * chunk + 2 * way + 1, pl.ds(row, 8), :] = own[8:]

    def halo_copies(c):
        groups = pl.ds(pl.multiple_of(c * (LANES // GROUP), LANES // GROUP), LANES // GROUP)
        return (
            remote(u_edge.at[c], u_halo_ref.at[groups], halo_sems.at[0, c], halo_sems.at[1, c], "ctx", after),
            remote(e_edge.at[c], e_halo_ref.at[groups], halo_sems.at[2, c], halo_sems.at[3, c], "ctx", before),
        )

    @pl.when(seq == seqs - 1)
    def _():
        for part in range(4):
            peer = quarter * chunk + part

            @pl.when(peer != me)
            def _():
                remote(states.at[peer], got.at[me], sems.at[0, peer], sems.at[1, me], "ctx", peer).start()

        for copy in halo_copies(chunk):
            copy.start()

    @pl.when(last_step)
    def _():
        got[pl.ds(me, 1)] = states[pl.ds(me, 1)]
        decay = jnp.exp(-float(length) * spread(rate_ref[...], me // quarter))
        decay = jnp.where(lax.rem(me, 2) == 0, decay[:8], decay[8:])
        decay = jnp.concatenate([decay] * 3, axis=0)
        forward = lax.rem(me, 4) < 2
        for step in range(1, count):
            peer = lax.rem(me + step, count)
            remote(states.at[peer], got.at[peer], sems.at[0, peer], sems.at[1, peer], "ctx", peer).wait_recv()
        running = jnp.zeros_like(decay)
        ahead = []
        for source in range(count):
            ahead.append(running)
            running = decay * running + got[source]
        running = jnp.zeros_like(decay)
        behind = [None] * count
        for source in reversed(range(count)):
            behind[source] = running
            running = decay * running + got[source]
        for target in range(count):
            scan[target] = jnp.where(forward, ahead[target], behind[target])
        for step in range(1, count):
            peer = lax.rem(me + step, count)
            remote(scan.at[peer], back.at[me], sems.at[2, peer], sems.at[3, me], "ctx", peer).start()
        back[pl.ds(me, 1)] = scan[pl.ds(me, 1)]
        for step in range(1, count):
            peer = lax.rem(me + step, count)
            remote(scan.at[peer], back.at[peer], sems.at[2, peer], sems.at[3, peer], "ctx", peer).wait_recv()
        carry_ref[...] = back[...]
        for step in range(1, count):
            peer = lax.rem(me + step, count)
            remote(states.at[peer], got.at[me], sems.at[0, peer], sems.at[1, me], "ctx", peer).wait_send()
            remote(scan.at[peer], back.at[me], sems.at[2, peer], sems.at[3, me], "ctx", peer).wait_send()
        for c in range(4):
            for copy in halo_copies(c):
                copy.wait()


def slanted(row, first_zero=False):
    lane = lax.broadcasted_iota(jnp.int32, (LANES, LANES), 1)
    here = lane >= lax.broadcasted_iota(jnp.int32, (LANES, LANES), 0)
    tiles = []
    earlier = jnp.zeros((LANES, LANES), f32)
    for j in range(row.shape[1] // LANES):
        part = jnp.broadcast_to(row[:, LANES * j : LANES * (j + 1)], (LANES, LANES))
        moved = pltpu.roll(part, 0, 1, stride=1, stride_axis=0)
        tiles.append(jnp.where(here, moved, earlier).astype(bf16))
        earlier = moved
    return tiles, jnp.where(here, 0.0, earlier).astype(bf16)


def split(value):
    high = value.astype(bf16)
    return high, (value - high.astype(f32)).astype(bf16)


def long_kernel(u_ref, u_halo_ref, e_ref, e_halo_ref, carry_ref, rate_ref, residue_ref, tap_ref, s_ref, w_ref, lag_ref, turned_ref):
    chunk = pl.program_id(0)
    place = lax.axis_index("ctx")
    count = lax.axis_size("ctx")
    length = u_ref.shape[3]
    half = length // 2
    per_step = u_ref.shape[0]
    rows = 3 * GROUP
    has_prev = place > 0
    has_next = place < count - 1
    parts = []
    for way in range(2):
        for seq in range(3):
            parts += [carry_ref[2 * way, 8 * seq : 8 * seq + 8], carry_ref[2 * way + 1, 8 * seq : 8 * seq + 8]]
    turned_ref[...] = jnp.concatenate(parts, axis=0).T
    zero = jnp.zeros((LANES, LANES), bf16)
    eye = group_mask((POLES, POLES), 1, 1)
    batch = 4

    def lanes(shape):
        return lax.broadcasted_iota(jnp.int32, shape, 1).astype(f32)

    def one(index):
        group = chunk * per_step + index
        pick = lax.broadcasted_iota(jnp.int32, rate_ref.shape, 1) == group
        rate = jnp.sum(jnp.where(pick, rate_ref[...], 0.0), axis=1, keepdims=True)
        residue = jnp.sum(jnp.where(pick, residue_ref[...], 0.0), axis=1, keepdims=True)
        rate_row = jnp.sum(jnp.where(eye, rate, 0.0), axis=0, keepdims=True)
        carry = turned_ref[pl.ds(pl.multiple_of(index * GROUP, GROUP), GROUP), :]
        ahead = jnp.concatenate([carry[:, POLES * j : POLES * (j + 1)] for j in range(3)], axis=0)
        behind = jnp.concatenate([carry[:, POLES * j : POLES * (j + 1)] for j in range(3, 6)], axis=0)
        u_halo = jnp.where(has_prev, u_halo_ref[index].reshape(rows, LANES), jnp.zeros((), bf16))
        e_halo = jnp.where(has_next, e_halo_ref[index].reshape(rows, LANES), jnp.zeros((), bf16))
        u_own = u_ref[index].reshape(rows, length)
        e_own = e_ref[index].reshape(rows, length)
        u_ext = jnp.concatenate([u_halo, u_own], axis=1)
        edge = lanes((POLES, LANES))

        def local_state(value, ago):
            high, low = split(jnp.exp(-rate * ago))
            return matmul(jnp.concatenate([value, value], axis=1), jnp.concatenate([high, low], axis=1), NT)

        def columns(parts):
            values = [split(part) for part in parts]
            high = jnp.concatenate([value[0] for value in values], axis=0)
            low = jnp.concatenate([value[1] for value in values], axis=0)
            return jnp.concatenate([high, low, high], axis=1)

        def weights(value):
            high, low = split(value)
            return jnp.concatenate([high, high, low], axis=0)

        yield
        near = jnp.exp(-float(half) * rate_row)
        ahead = ahead - local_state(u_halo, (LANES - 1.0) - edge)
        ahead_columns = columns([ahead, ahead * near])
        far = (behind - local_state(e_halo, edge)) * jnp.exp(float(half) * rate_row)
        behind_columns = columns([behind * near, behind, far])

        yield
        lag = lanes((POLES, 5 * LANES))
        h_row = jnp.sum(residue * jnp.exp(-rate * lag), axis=0, keepdims=True)
        h_tiles, _ = slanted(h_row)
        yield
        taps = tap_ref[pl.ds(group, 1), :].astype(f32)
        q = matmul(jnp.broadcast_to(taps, (16, LANES)).astype(bf16), jnp.concatenate(h_tiles, axis=1))[:1]
        yield
        q_tiles, _ = slanted(q)
        k_tiles, k_last = slanted(taps)
        k_tile = k_tiles[0]

        yield
        moment = jnp.sum(taps * jnp.exp(rate * edge), axis=1, keepdims=True)
        time = lanes((POLES, half))
        ahead_weights = weights(residue * moment * jnp.exp(-rate * (time + 1.0)))
        behind_weights = weights(residue * jnp.exp(-rate * (half - time)))

        yield
        left = jnp.concatenate([jnp.concatenate([jnp.zeros((rows, half), bf16), u_ext[:, : 3 * LANES]], axis=1), u_ext], axis=0)
        left_tiles = [zero] + q_tiles
        right = jnp.concatenate(
            [jnp.concatenate([left_tiles[4 - b], left_tiles[5 - b]], axis=1) for b in range(5)], axis=0
        )
        s = matmul(left, right) + matmul(ahead_columns, ahead_weights)
        s_ref[index] = jnp.concatenate([s[:rows], s[rows:]], axis=1).reshape(3, GROUP, length)

        yield
        left = jnp.concatenate(
            [
                e_own,
                jnp.concatenate([e_own[:, half:], jnp.zeros((rows, half), bf16)], axis=1),
                jnp.concatenate([e_halo, jnp.zeros((rows, length - LANES), bf16)], axis=1),
            ],
            axis=0,
        )
        right = jnp.concatenate(
            [jnp.concatenate(h_tiles[:4], axis=1), jnp.concatenate([zero] + h_tiles[:3], axis=1)], axis=0
        )
        p = matmul(left, right, NT) + matmul(behind_columns, behind_weights)
        tail = jnp.where(has_next, p[2 * rows :, :LANES], 0.0)
        p = jnp.concatenate([p[:rows], p[rows : 2 * rows], tail], axis=1).astype(bf16)

        yield
        left = jnp.concatenate([p[:, : 3 * LANES], p[:, half:]], axis=0)
        right = jnp.concatenate(
            [jnp.concatenate([k_tile, k_last, zero], axis=1), jnp.concatenate([zero, k_tile, k_last], axis=1)], axis=0
        )
        w = matmul(left, right, NT)
        w_ref[index] = jnp.concatenate([w[:rows], w[rows:]], axis=1).reshape(3, GROUP, length)

        yield
        p_stack = jnp.concatenate([p[:, LANES * b : LANES * (b + 1)] for b in range(4)], axis=0)
        u_stack = jnp.concatenate([u_ext[:, LANES * b : LANES * (b + 2)] for b in range(4)], axis=0)
        table = matmul(p_stack.T, u_stack)
        yield
        total = table[LANES - 8 :]
        for tile in reversed(range(LANES // 8 - 1)):
            total = pltpu.roll(total, 2 * LANES - 8, 1) + table[8 * tile : 8 * tile + 8]
        sub = lax.broadcasted_iota(jnp.int32, total.shape, 0)
        for bit in (1, 2, 4):
            total = jnp.where((sub & bit) > 0, pltpu.roll(total, 2 * LANES - bit, 1), total)
        total = jnp.sum(total, axis=0, keepdims=True)
        lag_ref[index] = pltpu.roll(total, 2 * LANES - 1, 1)[:, :LANES]

    def body(step, carry):
        for _ in zip_longest(*[one(batch * step + k) for k in range(batch)]):
            pass
        return carry

    lax.fori_loop(0, per_step // batch, body, 0)


def back_kernel(short_ref, stream_ref, prev_ref, tap_ref, cot_ref, s_ref, w_ref, out_ref, grad_ref, head_ref, tail_ref, corr_ref,
                rows_ref, g_ref, s_rows, w_rows, acc_ref):
    chunk = pl.program_id(0)
    seq = pl.program_id(1)
    length = stream_ref.shape[2]
    block = 64

    @pl.when(seq == 0)
    def _():
        acc_ref[...] = jnp.zeros_like(acc_ref)

    for stream in range(3):
        fill_rows(rows_ref, stream_ref, prev_ref[stream, 0], stream)
        g_ref[stream, length:] = jnp.zeros((HALO, LANES), f32)
    s_rows[...] = s_ref[:, 0].reshape(LANES, length).T
    w_rows[...] = w_ref[:, 0].reshape(LANES, length).T
    for first in range(0, length, block):
        here = slice(first, first + block)
        s = s_rows[here]
        w = w_rows[here]
        cot = cot_ref[0, here].astype(f32)
        out_ref[0, here] = (short_ref[0, 0, here] * s).astype(bf16)
        g_ref[0, here] = cot * s
        g_ref[1, here] = w * short_ref[2, 0, here]
        g_ref[2, here] = w * short_ref[1, 0, here]
    for stream in range(3):
        head_ref[stream, 0] = g_ref[stream, :HALO].astype(bf16)
        for first in range(0, length, block):
            total = None
            own = g_ref[stream, first : first + block]
            for offset in range(SHORT):
                term = tap_ref[stream, offset : offset + 1, :] * g_ref[stream, first + offset : first + offset + block]
                total = term if total is None else total + term
                begin = first + HALO - offset
                part = (own * rows_ref[stream, begin : begin + block]).reshape(block // 8, 8, LANES).sum(axis=0)
                acc_ref[stream, offset] += part
            grad_ref[stream, 0, first : first + block] = total.astype(bf16)
            if first + block == length:
                tail_ref[stream, 0] = total[block - HALO :]

    @pl.when(seq == pl.num_programs(1) - 1)
    def _():
        lane = lax.broadcasted_iota(jnp.int32, (LANES, LANES), 0) // GROUP + chunk * (LANES // GROUP)
        pick = jnp.where(lane == lax.broadcasted_iota(jnp.int32, (LANES, LANES), 1), 1.0, 0.0)
        sums = acc_ref[...].sum(axis=2).reshape(3 * 8, LANES)
        value = matmul(sums, pick, precision=highest)

        @pl.when(chunk == 0)
        def _():
            corr_ref[...] = value

        @pl.when(chunk > 0)
        def _():
            corr_ref[...] += value


def reduce_kernel(count, across, corr_ref, lag_ref, head_ref, corr_out, lag_out, head_out, mine, row_got, row_sum, col_got, norm_mine, norm_got,
                  row_sems, col_sems, norm_sems, head_sems):
    inner = 4
    me = lax.axis_index("ctx")
    ch = lax.axis_index("ch")
    col = lax.rem(me, inner)
    row = me // inner
    before = lax.rem(me + count - 1, count)
    after = lax.rem(me + 1, count)
    outer = count // inner

    def in_row(step):
        place = lax.rem(col + step, inner)
        return place, row * inner + place

    def in_col(step):
        place = lax.rem(row + step, outer)
        return place, place * inner + col

    def in_ch(step):
        place = lax.rem(ch + step, across)
        return place, place

    barrier = pltpu.get_barrier_semaphore()
    peers = [in_row(step)[1] for step in range(1, inner)] + [in_col(step)[1] for step in range(1, outer)] + [before, after]
    for peer in peers:
        pl.semaphore_signal(barrier, inc=1, device_id={"ctx": peer}, device_id_type=MESH)
    for step in range(1, across):
        pl.semaphore_signal(barrier, inc=1, device_id={"ch": in_ch(step)[1]}, device_id_type=MESH)
    pl.semaphore_wait(barrier, len(peers) + across - 1)
    top = corr_ref.shape[0]
    mine[:top] = corr_ref[...]
    mine[top:] = lag_ref[...]

    def gather(source, target, sems, axis, size, here, peer_of, between=None):
        copies = []
        for step in range(1, size):
            place, peer = peer_of(step)
            copies.append(remote(source, target.at[here], sems.at[0, place], sems.at[1, here], axis, peer))
        for copy in copies:
            copy.start()
        if between is not None:
            between()
        target[pl.ds(here, 1)] = source[...][None]
        for step in range(1, size):
            place, peer = peer_of(step)
            remote(source, target.at[place], sems.at[0, place], sems.at[1, place], axis, peer).wait_recv()
        total = target[0]
        for place in range(1, size):
            total = total + target[place]
        return total, copies

    head = remote(head_ref, head_out, head_sems.at[0], head_sems.at[1], "ctx", before)
    total, sent = gather(mine, row_got, row_sems, "ctx", inner, col, in_row, head.start)
    row_sum[...] = total
    total, more = gather(row_sum, col_got, col_sems, "ctx", outer, row, in_col)
    sent = sent + more
    norm_mine[...] = jnp.sum((total * total).reshape(total.shape[0] // 8, 8, LANES), axis=0)
    squares, more = gather(norm_mine, norm_got, norm_sems, "ch", across, ch, in_ch)
    sent = sent + more
    norm = jnp.sqrt(jnp.sum(jnp.sum(squares, axis=1, keepdims=True), axis=0, keepdims=True))
    factor = jnp.minimum(1.0, clip_norm / (norm + 1e-06))
    corr_out[...] = (total[:top] * factor).reshape(3, 8, LANES)[:, :SHORT, : corr_out.shape[2]]
    turn = lax.broadcasted_iota(jnp.int32, (LANES, LANES), 0) + lax.broadcasted_iota(jnp.int32, (LANES, LANES), 1) == LANES - 1
    lag_out[...] = matmul(total[top:] * factor, jnp.where(turn, 1.0, 0.0), precision=highest)
    for copy in sent:
        copy.wait_send()
    head.wait()


def edge_kernel(grad_ref, tail_ref, head_ref, tap_ref, out_ref):
    has_next = lax.axis_index("ctx") < lax.axis_size("ctx") - 1
    for stream in range(3):
        for seq in range(3):
            head = jnp.where(has_next, head_ref[stream, seq].astype(f32), 0.0)
            wide = jnp.concatenate([jnp.zeros((HALO, head.shape[1]), f32), head], axis=0)
            total = tail_ref[stream, seq]
            for offset in range(1, SHORT):
                total = total + tap_ref[stream, offset : offset + 1, :] * wide[offset : offset + HALO]
            low = jnp.concatenate([jnp.zeros_like(total), total], axis=0).astype(bf16)
            keep = lax.broadcasted_iota(jnp.int32, low.shape, 0) < HALO
            out_ref[stream, seq] = jnp.where(keep, grad_ref[stream, seq], low)


def params(**more):
    return pltpu.CompilerParams(vmem_limit_bytes=VMEM_LIMIT, **more)


def on_device(streams, short_filter, medium_filter, rates, residues, cotangent):
    count = lax.axis_size("ctx")
    across = lax.axis_size("ch")
    seqs, length, width = streams.shape[1:]
    groups = width // GROUP
    chunks = width // LANES
    per_chunk = LANES // GROUP
    shape = jax.ShapeDtypeStruct
    vmem = pl.BlockSpec(memory_space=pltpu.VMEM)
    anywhere = pl.BlockSpec(memory_space=pl.ANY)
    whole = lambda *dims: pl.BlockSpec(dims, lambda *steps: (0,) * len(dims))

    chunk_block = lambda c, k: (0, k, 0, c)
    turned_block = lambda c, k: (c, k, 0, 0)
    stream_spec = pl.BlockSpec((3, 1, length, LANES), chunk_block)
    prev_spec = pl.BlockSpec((3, 1, HALO, LANES), chunk_block)
    tap_spec = pl.BlockSpec((3, 8, LANES), lambda c, k: (0, 0, c))
    cot_spec = pl.BlockSpec((1, length, LANES), lambda c, k: (k, 0, c))
    turned_spec = pl.BlockSpec((per_chunk, 1, GROUP, length), turned_block)
    edge_shape = (3, seqs, HALO, width)
    slots = (count, 3 * 8, LANES)
    halo_shape = shape((groups, seqs, GROUP, LANES), bf16)

    short_sums, u, e, prev, taps, carry, u_halo, e_halo = pl.pallas_call(
        functools.partial(front_kernel, count),
        grid=(chunks, seqs),
        in_specs=[stream_spec, anywhere, whole(*short_filter.shape), cot_spec, whole(*rates.shape)],
        out_specs=[
            stream_spec, turned_spec, turned_spec, whole(*edge_shape), tap_spec, whole(*slots), anywhere, anywhere,
        ],
        out_shape=[
            shape(streams.shape, f32),
            shape((groups, seqs, GROUP, length), bf16),
            shape((groups, seqs, GROUP, length), bf16),
            shape(edge_shape, f32),
            shape((3, 8, width), f32),
            shape(slots, f32),
            halo_shape,
            halo_shape,
        ],
        scratch_shapes=[
            pltpu.VMEM((3, length + HALO, LANES), f32),
            pltpu.VMEM((2, 2, LANES, length), bf16),
            pltpu.VMEM((24, groups), f32),
            pltpu.VMEM(edge_shape, bf16),
            pltpu.VMEM((chunks, per_chunk, seqs, GROUP, LANES), bf16),
            pltpu.VMEM((chunks, per_chunk, seqs, GROUP, LANES), bf16),
            pltpu.VMEM(slots, f32),
            pltpu.VMEM(slots, f32),
            pltpu.VMEM(slots, f32),
            pltpu.VMEM(slots, f32),
            pltpu.SemaphoreType.DMA((2,)),
            pltpu.SemaphoreType.DMA((4, chunks)),
            pltpu.SemaphoreType.DMA((4, count)),
        ],
        compiler_params=params(collective_id=0, has_side_effects=True),
        name="front",
    )(streams, streams, short_filter, cotangent, rates)

    own_spec = pl.BlockSpec((per_chunk, seqs, GROUP, length), lambda c: (c, 0, 0, 0))
    halo_spec = pl.BlockSpec((per_chunk, seqs, GROUP, LANES), lambda c: (c, 0, 0, 0))
    s, w, lags = pl.pallas_call(
        long_kernel,
        grid=(chunks,),
        in_specs=[
            own_spec, halo_spec, own_spec, halo_spec, pl.BlockSpec((4, 24, LANES), lambda c: (c, 0, 0)),
            whole(*rates.shape), whole(*rates.shape), whole(groups, MEDIUM),
        ],
        out_specs=[own_spec, own_spec, pl.BlockSpec((per_chunk, 1, LANES), lambda c: (c, 0, 0))],
        out_shape=[
            shape((groups, seqs, GROUP, length), f32),
            shape((groups, seqs, GROUP, length), f32),
            shape((groups, 1, LANES), f32),
        ],
        scratch_shapes=[pltpu.VMEM((LANES, 6 * POLES), f32)],
        compiler_params=params(),
        name="long",
    )(u, u_halo, e, e_halo, carry, rates, residues, medium_filter.astype(f32).T)

    filtered, grads, heads, tails, corr = pl.pallas_call(
        back_kernel,
        grid=(chunks, seqs),
        in_specs=[stream_spec, stream_spec, prev_spec, tap_spec, cot_spec, turned_spec, turned_spec],
        out_specs=[cot_spec, stream_spec, prev_spec, prev_spec, whole(24, LANES)],
        out_shape=[
            shape(cotangent.shape, bf16),
            shape(streams.shape, bf16),
            shape(edge_shape, bf16),
            shape(edge_shape, f32),
            shape((24, LANES), f32),
        ],
        scratch_shapes=[
            pltpu.VMEM((3, length + HALO, LANES), f32),
            pltpu.VMEM((3, length + HALO, LANES), f32),
            pltpu.VMEM((length, LANES), f32),
            pltpu.VMEM((length, LANES), f32),
            pltpu.VMEM((3, 8, 8, LANES), f32),
        ],
        compiler_params=params(),
        name="back",
    )(short_sums, streams, prev, taps, cotangent, s, w)

    sums = (24 + groups, LANES)
    short_grad, medium_grad, next_heads = pl.pallas_call(
        functools.partial(reduce_kernel, count, across),
        in_specs=[vmem, vmem, anywhere],
        out_specs=[vmem, vmem, anywhere],
        out_shape=[shape(short_filter.shape, f32), shape((groups, LANES), f32), shape(edge_shape, bf16)],
        scratch_shapes=[
            pltpu.VMEM(sums, f32),
            pltpu.VMEM((4,) + sums, f32),
            pltpu.VMEM(sums, f32),
            pltpu.VMEM((count // 4,) + sums, f32),
            pltpu.VMEM((8, LANES), f32),
            pltpu.VMEM((across, 8, LANES), f32),
            pltpu.SemaphoreType.DMA((2, 4)),
            pltpu.SemaphoreType.DMA((2, count // 4)),
            pltpu.SemaphoreType.DMA((2, across)),
            pltpu.SemaphoreType.DMA((2,)),
        ],
        compiler_params=pltpu.CompilerParams(collective_id=1, has_side_effects=True),
        name="reduce",
    )(corr, lags.reshape(groups, LANES), heads)

    last = length // (2 * HALO) - 1
    last_spec = pl.BlockSpec((3, seqs, 2 * HALO, width), lambda i: (0, 0, last, 0))
    grads = pl.pallas_call(
        edge_kernel,
        grid=(1,),
        in_specs=[last_spec, whole(*edge_shape), whole(*edge_shape), whole(3, 8, width)],
        out_specs=last_spec,
        out_shape=shape(grads.shape, bf16),
        input_output_aliases={0: 0},
        compiler_params=params(),
        name="edge",
    )(grads, tails, next_heads, taps)
    return filtered, grads, short_grad, medium_grad.T


def solution(mesh):
    in_specs = (
        P(None, None, "ctx", "ch"),
        P(None, None, "ch"),
        P(None, "ch"),
        P(None, "ch"),
        P(None, "ch"),
        P(None, "ctx", "ch"),
    )
    out_specs = (
        P(None, "ctx", "ch"),
        P(None, None, "ctx", "ch"),
        P(None, None, "ch"),
        P(None, "ch"),
    )
    return jax.shard_map(on_device, mesh=mesh, in_specs=in_specs, out_specs=out_specs, check_vma=False)
```
